32 devices in a mesh: tm: 8 (over z, y), space: 4 (over x, core).
Axes of the slice: x: 2, y: 2, z: 4, core: 2. Of those that a mesh axis runs over, the one named last changes fastest.
Arguments:
- volume: float32 [8, 16, 256, 256], P('tm', 'space'), may hold values from -6 to 6
- prior_image: float32 [8, 16, 256, 256], P('tm', 'space'), may hold values from -6 to 6
- dual_pairs: float32 [8, 4, 16, 256, 256], P('tm', None, 'space'), may hold values from -0.3 to 0.3
- pair_cycle: int32 [8, 4], P('tm'), may hold values from -2 to 2, as said below
- pair_offset: int32 [8, 4], P('tm'), may hold values from -3 to 3
Outputs:
- volume_next: float32 [8, 16, 256, 256], P('tm', 'space')
- dual_next: float32 [8, 4, 16, 256, 256], P('tm', None, 'space')
The draws below stay inside these ranges and needn't reach their ends.
Inputs may be any that keep to these rules, and one draw needn't show every extreme that they name: `pair_cycle`: each frame has at least one filled slot; filled slots come first, name distinct cycle offsets, and always name a partner frame inside 0 .. 7.
All inputs are finite; a program needn't handle non-finite values.
Results may differ from the reference program's by a relative error of at most 0.0003.
Values sent between devices are 32-bit elements; how exact they have to be, the bound alone decides.
No kernel may reach another device: no remote copies, remote signals or barrier semaphores. Data moves between devices by JAX's collectives and lax.ppermute only.
A program may use at most 64 MiB of HBM per device.

```python
import jax
import jax.numpy as jnp
from jax import lax

NY = 256
NX = 256
PAIRS = 4
CYCLES = 8
FRAMES = 8
Z = 16


def draw_pair_cycle(key, part):
    stride = FRAMES // CYCLES
    frames = jnp.arange(FRAMES, dtype=jnp.int32)[:, None]
    hop_table = jnp.array([-2, -1, 1, 2], jnp.int32)[None, :]
    target_frame = frames + hop_table * stride
    validity = ((target_frame >= 0) & (target_frame < FRAMES)).astype(jnp.int32)
    order_key = jax.random.fold_in(key, 11)
    count_key = jax.random.fold_in(key, 23)
    row_keys = jax.random.split(order_key, FRAMES)
    priority = jax.vmap(lambda subkey: jax.random.permutation(subkey, 4))(row_keys).astype(jnp.int32)
    scores = validity * 8 + priority
    ranking = jnp.argsort(-scores, axis=1)
    live_count = jax.random.randint(count_key, (FRAMES, 1), 1, 5).astype(jnp.int32)
    live_count = jnp.minimum(live_count, jnp.sum(validity, axis=1, keepdims=True))
    picked = jnp.take_along_axis(hop_table * jnp.ones_like(validity), ranking, axis=1)
    slot_index = jnp.arange(4, dtype=jnp.int32)[None, :]
    return jnp.where(slot_index < live_count, picked, 0).astype(jnp.int32)


def with_ends(result, key, low, high):
    longest = result.shape.index(max(result.shape))
    spots = []
    for shift in (0, 1):
        where = [jax.random.randint(jax.random.fold_in(key, axis), (), 0, length) for axis, length in enumerate(result.shape)]
        where[longest] = (where[longest] + shift) % result.shape[longest]
        spots.append(tuple(where))
    return result.at[spots[0]].set(low).at[spots[1]].set(high)


def levels(stream_key, shape, pieces, low, high):
    gain = 1.0
    for dim, blocks in pieces:
        steps = jax.random.uniform(jax.random.fold_in(jax.random.fold_in(stream_key, 6), dim), (blocks,), jnp.float32, low / len(pieces), high / len(pieces))
        gain = gain * jnp.repeat(jnp.exp(steps), shape[dim] // blocks).reshape((-1,) + (1,) * (len(shape) - 1 - dim))
    return gain


def centred(own_key, shape, spread, bound, pieces=(), held_as=jnp.bfloat16):
    drawn = spread * jax.random.normal(own_key, shape, jnp.float32)
    if pieces:
        drawn = drawn * levels(own_key, shape, pieces, -0.22, 0.18)
    return jnp.clip(drawn, -bound, bound).astype(held_as)


def setup_inputs(seed: int = 0) -> dict:
    keys = jax.random.split(jax.random.key(seed), 6)
    volume = centred(keys[0], (FRAMES, Z, NY, NX), 1.0, 6.0, ((0, 8), (1, 4)), jnp.float32)
    prior_image = centred(keys[1], (FRAMES, Z, NY, NX), 1.0, 6.0, ((0, 8), (1, 4)), jnp.float32)
    dual_pairs = jnp.clip(jax.random.uniform(keys[2], (FRAMES, PAIRS, Z, NY, NX), jnp.float32, -0.3, 0.3) * levels(keys[2], (FRAMES, PAIRS, Z, NY, NX), ((0, 8), (2, 4)), -0.4, 0.0), -0.3, 0.3)
    pair_cycle = draw_pair_cycle(jax.random.fold_in(keys[5], 71), 0)
    pair_offset = with_ends(jax.random.randint(keys[4], (FRAMES, PAIRS), -3, 4), jax.random.fold_in(keys[4], 1), -3, 3).astype(jnp.int32)
    return {"volume": volume, "prior_image": prior_image, "dual_pairs": dual_pairs, "pair_cycle": pair_cycle, "pair_offset": pair_offset}


dual_step = 0.5
primal_step = 0.25
dual_bound = 0.3
fidelity = 1.0


def shift_rows(field, offset):
    lead = [(0, 0)] * (field.ndim - 2)
    padded = jnp.pad(field, lead + [(3, 3), (0, 0)])
    start = (3 - offset).astype(jnp.int32)
    return lax.dynamic_slice_in_dim(padded, start, field.shape[-2], field.ndim - 2)


def unshift_rows(field, offset):
    lead = [(0, 0)] * (field.ndim - 2)
    padded = jnp.pad(field, lead + [(3, 3), (0, 0)])
    start = (3 + offset).astype(jnp.int32)
    return lax.dynamic_slice_in_dim(padded, start, field.shape[-2], field.ndim - 2)


def box_mean(field):
    zsum = field[..., :-2, :, :] + field[..., 1:-1, :, :] + field[..., 2:, :, :]
    lead = [(0, 0)] * (zsum.ndim - 2)
    padded = jnp.pad(zsum, lead + [(1, 1), (0, 0)])
    ysum = padded[..., :-2, :] + padded[..., 1:-1, :] + padded[..., 2:, :]
    padded = jnp.pad(ysum, [(0, 0)] * (ysum.ndim - 1) + [(1, 1)])
    return (padded[..., :-2] + padded[..., 1:-1] + padded[..., 2:]) / 27.0


def reference(volume, prior_image, dual_pairs, pair_cycle, pair_offset):
    stride = FRAMES // CYCLES

    def frame_step(frame):
        current = volume[frame]
        fresh_list = []
        outgoing_list = []
        local_sum = jnp.zeros_like(current)
        for slot in range(PAIRS):
            cycle = pair_cycle[frame, slot]
            active = cycle != 0
            target = jnp.clip(frame + cycle * stride, 0, FRAMES - 1).astype(jnp.int32)
            partner = jnp.where(active, volume[target], jnp.zeros_like(current))
            shifted = shift_rows(partner, pair_offset[frame, slot])
            contrast = shifted - current
            squares = jnp.pad(contrast * contrast, ((1, 1), (0, 0), (0, 0)))
            weight_root = jnp.exp(-box_mean(squares) / 4.0)
            fresh = jnp.clip(dual_pairs[frame, slot] + dual_step * weight_root * contrast, -dual_bound, dual_bound)
            fresh = jnp.where(active, fresh, jnp.zeros_like(fresh))
            flux = weight_root * fresh
            local_sum = local_sum + flux
            fresh_list.append(fresh)
            outgoing_list.append(unshift_rows(flux, pair_offset[frame, slot]))
        return jnp.stack(fresh_list), local_sum, jnp.stack(outgoing_list)

    frames = jnp.arange(FRAMES, dtype=jnp.int32)
    dual_next, local_sums, outgoing = lax.map(frame_step, frames)

    def gather_step(frame):
        incoming = jnp.zeros(volume.shape[1:], jnp.float32)
        for hop_count in (-2, -1, 1, 2):
            source = frame - hop_count * stride
            inside = (source >= 0) & (source < FRAMES)
            source_clip = jnp.clip(source, 0, FRAMES - 1).astype(jnp.int32)
            for slot in range(PAIRS):
                match = inside & (pair_cycle[source_clip, slot] == hop_count)
                incoming = incoming + jnp.where(match, outgoing[source_clip, slot], jnp.zeros_like(incoming))
        return incoming

    incoming = lax.map(gather_step, frames)
    volume_next = (volume - primal_step * (incoming - local_sums) + primal_step * fidelity * prior_image) / (1.0 + primal_step * fidelity)
    return volume_next, dual_next
```

```python
import functools

import jax
import jax.numpy as jnp
from jax import lax
from jax.experimental import pallas as pl
from jax.experimental.pallas import tpu as pltpu
from jax.sharding import PartitionSpec as P

CYCLES = 8
HOPS = (-2, -1, 1, 2)

dual_step = 0.5
primal_step = 0.25
dual_bound = 0.3
fidelity = 1.0
scale = 1.0 / (1.0 + primal_step * fidelity)
flow = primal_step * scale
patch = -1.0 / (27.0 * 4.0)


LANES = 128
STEP = 16
EDGE = 16
RIM = 8


def chosen(table, hop):
    slot = jnp.int32(0)
    filled = table[0] == hop
    for k in range(1, 4):
        hit = table[k] == hop
        slot = jnp.where(hit, k, slot)
        filled = filled | hit
    return slot, filled


def offset_of(table, hop):
    offset = jnp.int32(0)
    for k in range(4):
        offset = jnp.where(table[k] == hop, table[4 + k], offset)
    return offset


def home_slot(table, hop):
    slot, filled = chosen(table, hop)
    count = jnp.int32(0)
    for k in range(4):
        count = count + (table[k] != 0).astype(jnp.int32)
    for other in HOPS:
        _, other_filled = chosen(table, other)
        count = count + ((other < hop) & jnp.logical_not(other_filled)).astype(jnp.int32)
    return jnp.where(filled, slot, count), filled


def pack_kernel(table, hops, *refs):
    sources, outs, (held,) = refs[:4], refs[4:8], refs[8:]
    rows = sources[0].shape[2]
    for half in range(2):
        held[half, pl.ds(0, RIM), :] = jnp.zeros((RIM, LANES), jnp.float32)
        held[half, pl.ds(RIM + rows, RIM), :] = jnp.zeros((RIM, LANES), jnp.float32)
    for j in range(4):
        offset = offset_of(table, hops[j])
        for half in range(2):
            lanes = pl.ds(half * LANES, LANES)
            held[half, pl.ds(RIM, rows), :] = sources[j][0, 0, :, lanes]
            outs[j][0, :, lanes] = held[half, pl.ds(RIM + offset, rows), :]


def pack(table, hops, dual):
    slots, depth, rows, columns = dual.shape
    spec = lambda j: pl.BlockSpec(
        (1, 1, rows, columns), lambda z, t, h: (chosen(t, h[j])[0], z, 0, 0)
    )
    return pl.pallas_call(
        pack_kernel,
        name="pack",
        grid_spec=pltpu.PrefetchScalarGridSpec(
            num_scalar_prefetch=2,
            grid=(depth,),
            in_specs=[spec(j) for j in range(4)],
            out_specs=[pl.BlockSpec((1, rows, columns), lambda z, t, h: (z, 0, 0))] * 4,
            scratch_shapes=[pltpu.VMEM((2, rows + 2 * RIM, LANES), jnp.float32)],
        ),
        out_shape=[jax.ShapeDtypeStruct((depth, rows, columns), jnp.float32)] * 4,
        cost_estimate=pl.CostEstimate(flops=0, bytes_accessed=8 * 4 * depth * rows * columns, transcendentals=0),
    )(table, hops, dual, dual, dual, dual)


def box_rows(sums, z, half, start):
    return (
        sums[z, half, pl.ds(start - 1, STEP), :]
        + sums[z, half, pl.ds(start, STEP), :]
        + sums[z, half, pl.ds(start + 1, STEP), :]
    )


def box_lanes(left, right, lane):
    zero = jnp.zeros_like(left)
    left_up, right_up = pltpu.roll(left, 1, 1), pltpu.roll(right, 1, 1)
    left_down, right_down = pltpu.roll(left, LANES - 1, 1), pltpu.roll(right, LANES - 1, 1)
    first, last = lane == 0, lane == LANES - 1
    return (
        left + jnp.where(first, zero, left_up) + jnp.where(last, right_down, left_down),
        right + jnp.where(first, left_up, right_up) + jnp.where(last, zero, right_down),
    )


def pair_kernel(places, first, hops, table, *refs):
    count = len(places)
    refs = list(refs)
    take = lambda k: [refs.pop(0) for _ in range(k)]
    tables = take(count)
    image, above, below = take(3)
    partners = take(count)
    heads, tails = take(2)
    dual, start = take(2)
    if not first:
        take(1)
    fresh_out, total_out = take(2)
    weight_outs = take(count)
    gain_outs = take(count)
    own, held, own_sums, in_sums, dual_in, fresh, weights, gains, total, sems, out_sems = refs
    depth, rows, columns = image.shape

    def copies(i):
        place, stacked = places[i]
        slot, _ = chosen(table, hops[place])
        moves = []
        for half in range(2):
            lanes = pl.ds(half * LANES, LANES)
            moves.append((partners[i].at[:, :, lanes], held.at[i, pl.ds(1, depth), half, pl.ds(EDGE, rows), :]))
            moves.append((tails.at[stacked, :, lanes], held.at[i, 0, half, pl.ds(EDGE, rows), :]))
            moves.append((heads.at[stacked, :, lanes], held.at[i, depth + 1, half, pl.ds(EDGE, rows), :]))
        moves.append((dual.at[slot], dual_in.at[i]))
        return [pltpu.make_async_copy(a, b, sems.at[7 * i + j]) for j, (a, b) in enumerate(moves)]

    base = 7 * count
    common = [
        pltpu.make_async_copy(image, own.at[pl.ds(1, depth), pl.ds(RIM, rows), :], sems.at[base]),
        pltpu.make_async_copy(above.at[0], own.at[0, pl.ds(RIM, rows), :], sems.at[base + 1]),
        pltpu.make_async_copy(below.at[0], own.at[depth + 1, pl.ds(RIM, rows), :], sems.at[base + 2]),
        pltpu.make_async_copy(start, total, sems.at[base + 3]),
    ]
    for c in common:
        c.start()
    incoming_copies = [copies(i) for i in range(count)]
    for group in incoming_copies:
        for c in group:
            c.start()

    for z in range(depth + 2):
        own[z, pl.ds(0, RIM), :] = jnp.zeros((RIM, columns), jnp.float32)
        own[z, pl.ds(RIM + rows, RIM), :] = jnp.zeros((RIM, columns), jnp.float32)
        for half in range(2):
            for i in range(count):
                held[i, z, half, pl.ds(0, EDGE), :] = jnp.zeros((EDGE, LANES), jnp.float32)
                held[i, z, half, pl.ds(EDGE + rows, EDGE), :] = jnp.zeros((EDGE, LANES), jnp.float32)
    for z in range(depth):
        for half in range(2):
            own_sums[z, half, pl.ds(0, RIM), :] = jnp.zeros((RIM, LANES), jnp.float32)
            own_sums[z, half, pl.ds(RIM + rows, RIM), :] = jnp.zeros((RIM, LANES), jnp.float32)

    row = lax.broadcasted_iota(jnp.int32, (STEP, LANES), 0)
    lane = lax.broadcasted_iota(jnp.int32, (STEP, LANES), 1)

    for c in common:
        c.wait()

    out_copies = []
    for i in range(count):
        place, _ = places[i]
        hop = hops[place]
        own_offset = offset_of(table, hop)
        slot, filled = home_slot(table, hop)
        bound = jnp.where(filled, jnp.float32(dual_bound), jnp.float32(0.0))
        _, in_filled = chosen(tables[i], -hop)
        in_offset = offset_of(tables[i], -hop)
        low = jnp.where(in_filled, -in_offset, 4 * rows)
        high = rows - 1 - in_offset
        for c in incoming_copies[i]:
            c.wait()

        def own_contrast(z, half, y):
            return held[i, z, half, pl.ds(EDGE + y - own_offset, STEP), :] - own[
                z, pl.ds(pl.multiple_of(RIM + y, 8), STEP), pl.ds(half * LANES, LANES)
            ]

        def in_contrast(z, half, y, inside):
            mine = own[z, pl.ds(pl.multiple_of(RIM + y, 8), STEP), pl.ds(half * LANES, LANES)]
            if inside is not None:
                mine = jnp.where(inside, mine, 0.0)
            return mine - held[i, z, half, pl.ds(EDGE + y + in_offset, STEP), :]

        def add_slices(sums, contrast, y):
            for half in range(2):
                squares = []
                for z in range(depth + 2):
                    value = contrast(z, half)
                    squares.append(value * value)
                for z in range(depth):
                    sums[z, half, pl.ds(pl.multiple_of(RIM + y, 8), STEP), :] = squares[z] + squares[z + 1] + squares[z + 2]

        def gather(step, carry):
            y = step * STEP
            add_slices(own_sums, lambda z, half: own_contrast(z, half, y), y)
            return carry

        def gather_in(step, carry):
            y = step * STEP - RIM
            inside = (row + y >= low) & (row + y <= high)
            add_slices(in_sums, lambda z, half: in_contrast(z, half, y, inside), y)
            return carry

        def apply(step, carry):
            y = pl.multiple_of(step * STEP, STEP)
            inside = (row + y >= low) & (row + y <= high)
            here = pl.ds(y, STEP)
            for z in range(depth):
                own_box = box_lanes(
                    box_rows(own_sums, z, 0, RIM + y), box_rows(own_sums, z, 1, RIM + y), lane
                )
                in_box = box_lanes(
                    box_rows(in_sums, z, 0, RIM + y), box_rows(in_sums, z, 1, RIM + y), lane
                )
                for half in range(2):
                    lanes = pl.ds(half * LANES, LANES)
                    weight = jnp.exp(own_box[half] * patch)
                    value = dual_in[i, z, here, lanes] + (dual_step * weight) * own_contrast(z + 1, half, y)
                    value = jnp.minimum(jnp.maximum(value, -bound), bound)
                    fresh[i, z, here, lanes] = value
                    flux = (weight * value) * flow
                    if first and i == 0:
                        mine = own[z + 1, pl.ds(pl.multiple_of(RIM + y, 8), STEP), lanes]
                        flux = flux + (scale * mine)
                        total[z, here, lanes] = (flow * fidelity) * total[z, here, lanes] + flux
                    else:
                        total[z, here, lanes] = total[z, here, lanes] + flux
                    weight = jnp.exp(in_box[half] * patch)
                    gain = (dual_step * weight) * in_contrast(z + 1, half, y, None)
                    weights[i, z, here, lanes] = jnp.where(inside, weight, 0.0)
                    gains[i, z, here, lanes] = gain
            return carry

        lax.fori_loop(0, rows // STEP, gather, 0)
        lax.fori_loop(0, (rows + 2 * RIM) // STEP, gather_in, 0)
        lax.fori_loop(0, rows // STEP, apply, 0)

        done = [
            pltpu.make_async_copy(fresh.at[i], fresh_out.at[slot], out_sems.at[3 * i]),
            pltpu.make_async_copy(weights.at[i], weight_outs[i], out_sems.at[3 * i + 1]),
            pltpu.make_async_copy(gains.at[i], gain_outs[i], out_sems.at[3 * i + 2]),
        ]
        if i == count - 1:
            done.append(pltpu.make_async_copy(total, total_out, out_sems.at[3 * count]))
        for c in done:
            c.start()
        out_copies += done
    for c in out_copies:
        c.wait()


def pairs(places, hops, table, tables, image, above, below, partners, heads, tails, dual, start, fresh=None):
    count = len(places)
    depth, rows, columns = image.shape
    first = fresh is None
    block = jax.ShapeDtypeStruct(image.shape, jnp.float32)
    any_spec = pl.BlockSpec(memory_space=pl.ANY)
    smem = pl.BlockSpec(memory_space=pltpu.SMEM)
    operands = [hops, table, *tables, image, above, below, *partners, heads, tails, dual, start]
    specs = [smem] * (2 + count) + [any_spec] * (len(operands) - 2 - count)
    aliases = {}
    if not first:
        aliases = {len(operands): 0}
        operands.append(fresh)
        specs.append(any_spec)
    f32 = jnp.float32
    cells = depth * rows * columns
    return pl.pallas_call(
        functools.partial(pair_kernel, places, first),
        name="pairs_first" if first else "pairs_last",
        in_specs=specs,
        out_specs=[any_spec] * (2 + 2 * count),
        out_shape=[jax.ShapeDtypeStruct(dual.shape, f32)] + [block] * (1 + 2 * count),
        input_output_aliases=aliases,
        scratch_shapes=[
            pltpu.VMEM((depth + 2, rows + 2 * RIM, columns), f32),
            pltpu.VMEM((count, depth + 2, 2, rows + 2 * EDGE, LANES), f32),
            pltpu.VMEM((depth, 2, rows + 2 * RIM, LANES), f32),
            pltpu.VMEM((depth, 2, rows + 2 * RIM, LANES), f32),
            pltpu.VMEM((count, depth, rows, columns), f32),
            pltpu.VMEM((count, depth, rows, columns), f32),
            pltpu.VMEM((count, depth, rows, columns), f32),
            pltpu.VMEM((count, depth, rows, columns), f32),
            pltpu.VMEM((depth, rows, columns), f32),
            pltpu.SemaphoreType.DMA((7 * count + 4,)),
            pltpu.SemaphoreType.DMA((3 * count + 1,)),
        ],
        cost_estimate=pl.CostEstimate(
            flops=count * 60 * cells, bytes_accessed=4 * (3 + 7 * count) * cells, transcendentals=2 * count * cells
        ),
    )(*operands)


def settle_kernel(count, total, *refs):
    duals, weights, gains, out = refs[:count], refs[count : 2 * count], refs[2 * count : 3 * count], refs[-1]
    arriving = jnp.zeros(total.shape, jnp.float32)
    for i in range(count):
        value = duals[i][...] + gains[i][...]
        value = jnp.minimum(jnp.maximum(value, -dual_bound), dual_bound)
        arriving = arriving + weights[i][...] * value
    out[...] = total[...] - flow * arriving


def settle(total, duals, weights, gains):
    depth, rows, columns = total.shape
    spec = pl.BlockSpec((1, rows // 2, columns), lambda z, r: (z, r, 0))
    count = len(duals)
    return pl.pallas_call(
        functools.partial(settle_kernel, count),
        name="settle%d" % count,
        grid=(depth, 2),
        in_specs=[spec] * (1 + 3 * count),
        out_specs=spec,
        out_shape=jax.ShapeDtypeStruct(total.shape, jnp.float32),
        cost_estimate=pl.CostEstimate(
            flops=5 * count * total.size, bytes_accessed=4 * (2 + 3 * count) * total.size, transcendentals=0
        ),
    )(total, *duals, *weights, *gains)


def shards(volume, prior_image, dual_pairs, pair_cycle, pair_offset):
    frames = lax.axis_size("tm")
    spaces = lax.axis_size("space")
    stride = frames // CYCLES
    image = volume[0]
    dual = dual_pairs[0]
    cycle_of = lambda t: t // stride
    every = range(frames)
    swap = [(t, t + stride if cycle_of(t) % 2 == 0 else t - stride) for t in every]
    cross = [(t, t - stride if cycle_of(t) % 2 == 0 else t + stride) for t in every]
    cross = [(a, b) for a, b in cross if 0 <= b < frames]
    later = [(t, t + 2 * stride) for t in every if t + 2 * stride < frames]
    sooner = [(t, t - 2 * stride) for t in every if t - 2 * stride >= 0]
    relay = [(t, t + 2 * stride if cycle_of(t) % 2 == 0 else t - 2 * stride) for t in every]
    relay = [(a, b) for a, b in relay if 0 <= b < frames]
    onward = [(s, s + 1) for s in range(spaces - 1)]
    backward = [(s + 1, s) for s in range(spaces - 1)]
    send = lambda x, pairs_: lax.ppermute(x, "tm", pairs_)

    parity = (lax.axis_index("tm") // stride) % 2
    near = (1 - 2 * parity).astype(jnp.int32)
    hops = jnp.stack([near, -near, jnp.int32(2), jnp.int32(-2)])
    table = jnp.concatenate([pair_cycle[0], pair_offset[0]])

    near_image = send(image, swap)
    before_image = send(image, later)
    after_image = send(image, sooner)
    above = lax.ppermute(image[-1:], "space", onward)
    below = lax.ppermute(image[:1], "space", backward)
    near_dual, far_dual, later_dual, sooner_dual = pack(table, hops, dual)
    near_dual = send(near_dual, swap)
    far_dual = send(far_dual, cross)
    near_table, far_table, before_table, after_table = (
        send(table, p) for p in (swap, cross, later, sooner)
    )
    far_image = send(near_image, relay)
    before_dual = send(later_dual, later)
    after_dual = send(sooner_dual, sooner)

    three = (near_image, after_image, before_image)
    tails = lax.ppermute(jnp.stack([x[-1] for x in three]), "space", onward)
    heads = lax.ppermute(jnp.stack([x[0] for x in three]), "space", backward)
    fresh, total, wn, wa, wb, gn, ga, gb = pairs(
        ((0, 0), (2, 1), (3, 2)),
        hops, table, (near_table, after_table, before_table), image, above, below,
        three, heads, tails, dual, prior_image[0],
    )
    far_tail = lax.ppermute(far_image[-1:], "space", onward)
    far_head = lax.ppermute(far_image[:1], "space", backward)
    fresh, total, wf, gf = pairs(
        ((1, 0),),
        hops, table, (far_table,), image, above, below,
        (far_image,), far_head, far_tail, dual, total, fresh,
    )
    total = settle(total, (near_dual,), (wn,), (gn,))
    volume_next = settle(total, (far_dual, after_dual, before_dual), (wf, wa, wb), (gf, ga, gb))
    return (volume_next[None], fresh[None])


def solution(mesh):
    return jax.shard_map(
        shards,
        mesh=mesh,
        in_specs=(
            P("tm", "space", None, None),
            P("tm", "space", None, None),
            P("tm", None, "space", None, None),
            P("tm", None),
            P("tm", None),
        ),
        out_specs=(P("tm", "space", None, None), P("tm", None, "space", None, None)),
        check_vma=False,
    )
```

```python
import functools

import jax
import jax.numpy as jnp
from jax import lax
from jax.experimental import pallas as pl
from jax.experimental.pallas import tpu as pltpu
from jax.sharding import PartitionSpec as P


CYCLES = 8
HOPS = (-2, -1, 1, 2)

dual_step = 0.5
primal_step = 0.25
dual_bound = 0.3
fidelity = 1.0
scale = 1.0 / (1.0 + primal_step * fidelity)
flow = primal_step * scale
patch = -1.0 / (27.0 * 4.0)

KEPT = jax.ShapeDtypeStruct


LANES = 128
STEP = 16
EDGE = 16
RIM = 8


def chosen(table, hop):
    slot = jnp.int32(0)
    filled = table[0] == hop
    for k in range(1, 4):
        hit = table[k] == hop
        slot = jnp.where(hit, k, slot)
        filled = filled | hit
    return slot, filled


def offset_of(table, hop):
    offset = jnp.int32(0)
    for k in range(4):
        offset = jnp.where(table[k] == hop, table[4 + k], offset)
    return offset


def home_slot(table, hop):
    slot, filled = chosen(table, hop)
    count = jnp.int32(0)
    for k in range(4):
        count = count + (table[k] != 0).astype(jnp.int32)
    for other in HOPS:
        _, other_filled = chosen(table, other)
        count = count + ((other < hop) & jnp.logical_not(other_filled)).astype(jnp.int32)
    return jnp.where(filled, slot, count), filled


def pack_kernel(table, hops, *refs):
    sources, outs, (held,) = refs[:4], refs[4:8], refs[8:]
    rows = sources[0].shape[2]
    for half in range(2):
        held[half, pl.ds(0, RIM), :] = jnp.zeros((RIM, LANES), jnp.float32)
        held[half, pl.ds(RIM + rows, RIM), :] = jnp.zeros((RIM, LANES), jnp.float32)
    for j in range(4):
        offset = offset_of(table, hops[j])
        for half in range(2):
            lanes = pl.ds(half * LANES, LANES)
            held[half, pl.ds(RIM, rows), :] = sources[j][0, 0, :, lanes]
            outs[j][0, :, lanes] = held[half, pl.ds(RIM + offset, rows), :]


def pack(table, hops, dual):
    _, depth, rows, columns = dual.shape
    spec = lambda j: pl.BlockSpec(
        (1, 1, rows, columns), lambda z, t, h: (chosen(t, h[j])[0], z, 0, 0)
    )
    return pl.pallas_call(
        pack_kernel,
        name="pack",
        grid_spec=pltpu.PrefetchScalarGridSpec(
            num_scalar_prefetch=2,
            grid=(depth,),
            in_specs=[spec(j) for j in range(4)],
            out_specs=[pl.BlockSpec((1, rows, columns), lambda z, t, h: (z, 0, 0))] * 4,
            scratch_shapes=[pltpu.VMEM((2, rows + 2 * RIM, LANES), jnp.float32)],
        ),
        out_shape=[jax.ShapeDtypeStruct((depth, rows, columns), jnp.float32)] * 4,
        cost_estimate=pl.CostEstimate(flops=0, bytes_accessed=8 * 4 * depth * rows * columns, transcendentals=0),
    )(table, hops, dual, dual, dual, dual)


def box_rows(sums, z, half, start):
    return (
        sums[z, half, pl.ds(start - 1, STEP), :]
        + sums[z, half, pl.ds(start, STEP), :]
        + sums[z, half, pl.ds(start + 1, STEP), :]
    )


def box_lanes(left, right, lane):
    zero = jnp.zeros_like(left)
    left_up, right_up = pltpu.roll(left, 1, 1), pltpu.roll(right, 1, 1)
    left_down, right_down = pltpu.roll(left, LANES - 1, 1), pltpu.roll(right, LANES - 1, 1)
    first, last = lane == 0, lane == LANES - 1
    return (
        left + jnp.where(first, zero, left_up) + jnp.where(last, right_down, left_down),
        right + jnp.where(first, left_up, right_up) + jnp.where(last, zero, right_down),
    )


def pair_kernel(places, first, depth, hops, table, *refs):
    count = len(places)
    refs = list(refs)
    take = lambda k: [refs.pop(0) for _ in range(k)]
    tables = take(count)
    image, above, below, dual, start = take(5)
    partners, tails, heads = take(count), take(count), take(count)
    if not first:
        take(1)
    fresh_out, total = take(2)
    weights, gains = take(count), take(count)
    own, held, own_sums, in_sums, dual_in, fresh, sems, out_sems = refs
    rows, columns = image.shape[1:]
    per = 7

    def copies(i):
        place, stacked = places[i]
        slot, _ = chosen(table, hops[place])
        moves = []
        for half in range(2):
            lanes = pl.ds(half * LANES, LANES)
            moves.append((partners[i].at[:, :, lanes], held.at[i, pl.ds(1, depth), half, pl.ds(EDGE, rows), :]))
            moves.append((tails[i].at[stacked, :, lanes], held.at[i, 0, half, pl.ds(EDGE, rows), :]))
            moves.append((heads[i].at[stacked, :, lanes], held.at[i, depth + 1, half, pl.ds(EDGE, rows), :]))
        moves.append((dual.at[slot], dual_in.at[i]))
        return [pltpu.make_async_copy(a, b, sems.at[per * i + j]) for j, (a, b) in enumerate(moves)]

    base = per * count
    common = [
        pltpu.make_async_copy(image, own.at[pl.ds(1, depth), pl.ds(RIM, rows), :], sems.at[base]),
        pltpu.make_async_copy(above.at[0], own.at[0, pl.ds(RIM, rows), :], sems.at[base + 1]),
        pltpu.make_async_copy(below.at[0], own.at[depth + 1, pl.ds(RIM, rows), :], sems.at[base + 2]),
        pltpu.make_async_copy(start, total, sems.at[base + 3]),
    ]
    for c in common:
        c.start()
    incoming_copies = [copies(i) for i in range(count)]
    for group in incoming_copies:
        for c in group:
            c.start()

    for z in range(depth + 2):
        own[z, pl.ds(0, RIM), :] = jnp.zeros((RIM, columns), jnp.float32)
        own[z, pl.ds(RIM + rows, RIM), :] = jnp.zeros((RIM, columns), jnp.float32)
        for half in range(2):
            for i in range(count):
                held[i, z, half, pl.ds(0, EDGE), :] = jnp.zeros((EDGE, LANES), jnp.float32)
                held[i, z, half, pl.ds(EDGE + rows, EDGE), :] = jnp.zeros((EDGE, LANES), jnp.float32)
    for z in range(depth):
        for half in range(2):
            own_sums[z, half, pl.ds(0, RIM), :] = jnp.zeros((RIM, LANES), jnp.float32)
            own_sums[z, half, pl.ds(RIM + rows, RIM), :] = jnp.zeros((RIM, LANES), jnp.float32)

    row = lax.broadcasted_iota(jnp.int32, (STEP, LANES), 0)
    lane = lax.broadcasted_iota(jnp.int32, (STEP, LANES), 1)

    for c in common:
        c.wait()

    out_copies = []
    for i in range(count):
        place, _ = places[i]
        hop = hops[place]
        own_offset = offset_of(table, hop)
        slot, filled = home_slot(table, hop)
        bound = jnp.where(filled, jnp.float32(dual_bound), jnp.float32(0.0))
        for c in incoming_copies[i]:
            c.wait()
        _, in_filled = chosen(tables[i], -hop)
        in_offset = offset_of(tables[i], -hop)
        low = jnp.where(in_filled, -in_offset, 4 * rows)
        high = rows - 1 - in_offset

        def own_contrast(z, half, y):
            return held[i, z, half, pl.ds(EDGE + y - own_offset, STEP), :] - own[
                z, pl.ds(pl.multiple_of(RIM + y, 8), STEP), pl.ds(half * LANES, LANES)
            ]

        def in_contrast(z, half, y, inside):
            mine = own[z, pl.ds(pl.multiple_of(RIM + y, 8), STEP), pl.ds(half * LANES, LANES)]
            if inside is not None:
                mine = jnp.where(inside, mine, 0.0)
            return mine - held[i, z, half, pl.ds(EDGE + y + in_offset, STEP), :]

        def add_slices(sums, contrast, y):
            for half in range(2):
                squares = []
                for z in range(depth + 2):
                    value = contrast(z, half)
                    squares.append(value * value)
                for z in range(depth):
                    sums[z, half, pl.ds(pl.multiple_of(RIM + y, 8), STEP), :] = squares[z] + squares[z + 1] + squares[z + 2]

        def gather(step, carry):
            y = step * STEP
            add_slices(own_sums, lambda z, half: own_contrast(z, half, y), y)
            return carry

        def gather_in(step, carry):
            y = step * STEP - RIM
            inside = (row + y >= low) & (row + y <= high)
            add_slices(in_sums, lambda z, half: in_contrast(z, half, y, inside), y)
            return carry

        def apply(step, carry):
            y = pl.multiple_of(step * STEP, STEP)
            inside = (row + y >= low) & (row + y <= high)
            here = pl.ds(y, STEP)
            for z in range(depth):
                own_box = box_lanes(
                    box_rows(own_sums, z, 0, RIM + y), box_rows(own_sums, z, 1, RIM + y), lane
                )
                in_box = box_lanes(
                    box_rows(in_sums, z, 0, RIM + y), box_rows(in_sums, z, 1, RIM + y), lane
                )
                for half in range(2):
                    lanes = pl.ds(half * LANES, LANES)
                    weight = jnp.exp(own_box[half] * patch)
                    value = dual_in[i, z, here, lanes] + (dual_step * weight) * own_contrast(z + 1, half, y)
                    value = jnp.minimum(jnp.maximum(value, -bound), bound)
                    fresh[i, z, here, lanes] = value
                    flux = (weight * value) * flow
                    if first and i == 0:
                        mine = own[z + 1, pl.ds(pl.multiple_of(RIM + y, 8), STEP), lanes]
                        flux = flux + (scale * mine)
                        total[z, here, lanes] = (flow * fidelity) * total[z, here, lanes] + flux
                    else:
                        total[z, here, lanes] = total[z, here, lanes] + flux
                    weight = jnp.exp(in_box[half] * patch)
                    gain = (dual_step * weight) * in_contrast(z + 1, half, y, None)
                    weights[i][z, here, lanes] = jnp.where(inside, weight, 0.0)
                    gains[i][z, here, lanes] = gain
            return carry

        lax.fori_loop(0, rows // STEP, gather, 0)
        lax.fori_loop(0, (rows + 2 * RIM) // STEP, gather_in, 0)
        lax.fori_loop(0, rows // STEP, apply, 0)

        done = pltpu.make_async_copy(fresh.at[i], fresh_out.at[slot], out_sems.at[i])
        done.start()
        out_copies.append(done)
    for c in out_copies:
        c.wait()


def pairs(places, hops, table, tables, image, above, below, dual, start, partners, tails, heads, fresh=None):
    count = len(places)
    depth, rows, columns = image.shape
    first = fresh is None
    f32 = jnp.float32
    block = KEPT(image.shape, f32)
    any_spec = pl.BlockSpec(memory_space=pl.ANY)
    vmem_spec = pl.BlockSpec(memory_space=pltpu.VMEM)
    smem = pl.BlockSpec(memory_space=pltpu.SMEM)
    operands = [hops, table, *tables, image, above, below, dual, start, *partners, *tails, *heads]
    specs = [smem] * (2 + count) + [any_spec] * (len(operands) - 2 - count)
    aliases = {}
    if not first:
        aliases = {len(operands): 0}
        operands.append(fresh)
        specs.append(any_spec)
    cells = depth * rows * columns
    return pl.pallas_call(
        functools.partial(pair_kernel, places, first, depth),
        name="pairs_first" if first else "pairs_last",
        in_specs=specs,
        out_specs=[any_spec] + [vmem_spec] * (1 + 2 * count),
        out_shape=[jax.ShapeDtypeStruct(dual.shape, f32)] + [block] * (1 + 2 * count),
        input_output_aliases=aliases,
        scratch_shapes=[
            pltpu.VMEM((depth + 2, rows + 2 * RIM, columns), f32),
            pltpu.VMEM((count, depth + 2, 2, rows + 2 * EDGE, LANES), f32),
            pltpu.VMEM((depth, 2, rows + 2 * RIM, LANES), f32),
            pltpu.VMEM((depth, 2, rows + 2 * RIM, LANES), f32),
            pltpu.VMEM((count, depth, rows, columns), f32),
            pltpu.VMEM((count, depth, rows, columns), f32),
            pltpu.SemaphoreType.DMA((7 * count + 4,)),
            pltpu.SemaphoreType.DMA((count,)),
        ],
        compiler_params=pltpu.CompilerParams(vmem_limit_bytes=28 << 20),
        cost_estimate=pl.CostEstimate(
            flops=count * 60 * cells, bytes_accessed=4 * (3 + 7 * count) * cells, transcendentals=2 * count * cells
        ),
    )(*operands)


def settle_kernel(count, total, *refs):
    duals, weights, gains, out = refs[:count], refs[count : 2 * count], refs[2 * count : 3 * count], refs[-1]
    depth, rows, _ = total.shape

    def body(step, carry):
        here = pl.ds(pl.multiple_of(step * STEP, STEP), STEP)
        for z in range(depth):
            arriving = None
            for i in range(count):
                value = duals[i][z, here, :] + gains[i][z, here, :]
                value = weights[i][z, here, :] * jnp.minimum(jnp.maximum(value, -dual_bound), dual_bound)
                arriving = value if arriving is None else arriving + value
            out[z, here, :] = total[z, here, :] - flow * arriving
        return carry

    lax.fori_loop(0, rows // STEP, body, 0)


def settle(total, duals, weights, gains, last):
    count = len(duals)
    vmem_spec = pl.BlockSpec(memory_space=pltpu.VMEM)
    return pl.pallas_call(
        functools.partial(settle_kernel, count),
        in_specs=[vmem_spec] * (1 + 3 * count),
        out_specs=vmem_spec,
        out_shape=(jax.ShapeDtypeStruct if last else KEPT)(total.shape, jnp.float32),
        compiler_params=pltpu.CompilerParams(vmem_limit_bytes=20 << 20),
        cost_estimate=pl.CostEstimate(
            flops=5 * count * total.size, bytes_accessed=4 * (2 + 3 * count) * total.size, transcendentals=0
        ),
    )(total, *duals, *weights, *gains)


def shards(volume, prior_image, dual_pairs, pair_cycle, pair_offset):
    frames = lax.axis_size("tm")
    spaces = lax.axis_size("space")
    stride = frames // CYCLES
    image = volume[0]
    dual = dual_pairs[0]
    cycle_of = lambda t: t // stride
    every = range(frames)
    swap = [(t, t + stride if cycle_of(t) % 2 == 0 else t - stride) for t in every]
    cross = [(t, t - stride if cycle_of(t) % 2 == 0 else t + stride) for t in every]
    cross = [(a, b) for a, b in cross if 0 <= b < frames]
    later = [(t, t + 2 * stride) for t in every if t + 2 * stride < frames]
    sooner = [(t, t - 2 * stride) for t in every if t - 2 * stride >= 0]
    relay = [(t, t + 2 * stride if cycle_of(t) % 2 == 0 else t - 2 * stride) for t in every]
    relay = [(a, b) for a, b in relay if 0 <= b < frames]
    onward = [(s, s + 1) for s in range(spaces - 1)]
    backward = [(s + 1, s) for s in range(spaces - 1)]

    def send(x, pairs_, axis="tm"):
        return lax.ppermute(x, axis, pairs_)

    parity = (lax.axis_index("tm") // stride) % 2
    near = (1 - 2 * parity).astype(jnp.int32)
    hops = jnp.stack([near, -near, jnp.int32(2), jnp.int32(-2)])
    table = jnp.concatenate([pair_cycle[0], pair_offset[0]])

    near_image = send(image, swap)
    before_image = send(image, later)
    after_image = send(image, sooner)
    near_dual, far_dual, later_dual, sooner_dual = pack(table, hops, dual)
    near_dual = send(near_dual, swap)
    far_dual = send(far_dual, cross)
    far_image = send(near_image, relay)
    near_table = send(table, swap)
    far_table = send(table, cross)
    before_table = send(table, later)
    after_table = send(table, sooner)

    stack = (image, near_image, after_image, before_image)
    bottoms = jnp.stack([x[-1] for x in stack])
    tops = jnp.stack([x[0] for x in stack])
    tails = send(bottoms, onward, "space")
    heads = send(tops, backward, "space")
    before_dual = send(later_dual, later)
    after_dual = send(sooner_dual, sooner)
    fresh, total, wn, wa, gn, ga = pairs(
        ((0, 1), (2, 2)), hops, table, (near_table, after_table), image, tails, heads, dual, prior_image[0],
        (near_image, after_image), (tails,) * 2, (heads,) * 2,
    )
    far_tail = send(far_image[-1:], onward, "space")
    far_head = send(far_image[:1], backward, "space")
    fresh, total, wb, wf, gb, gf = pairs(
        ((3, 3), (1, 0)), hops, table, (before_table, far_table), image, tails, heads, dual, total,
        (before_image, far_image), (tails, far_tail), (heads, far_head), fresh,
    )
    volume_next = settle(
        total, (near_dual, after_dual, before_dual, far_dual), (wn, wa, wb, wf), (gn, ga, gb, gf), True
    )
    return (volume_next[None], fresh[None])


def solution(mesh):
    return jax.shard_map(
        shards,
        mesh=mesh,
        in_specs=(
            P("tm", "space", None, None),
            P("tm", "space", None, None),
            P("tm", None, "space", None, None),
            P("tm", None),
            P("tm", None),
        ),
        out_specs=(P("tm", "space", None, None), P("tm", None, "space", None, None)),
        check_vma=False,
    )
```

```python
import functools

import jax
import jax.numpy as jnp
from jax import lax
from jax.experimental import pallas as pl
from jax.experimental.pallas import tpu as pltpu
from jax.sharding import PartitionSpec as P


CYCLES = 8
HOPS = (-2, -1, 1, 2)

dual_step = 0.5
primal_step = 0.25
dual_bound = 0.3
fidelity = 1.0
scale = 1.0 / (1.0 + primal_step * fidelity)
flow = primal_step * scale
patch = -1.0 / (27.0 * 4.0)


LANES = 128
STEP = 32
PARTS = 2
EDGE = 16
RIM = 8


def chosen(table, hop):
    slot = jnp.int32(0)
    filled = table[0] == hop
    for k in range(1, 4):
        hit = table[k] == hop
        slot = jnp.where(hit, k, slot)
        filled = filled | hit
    return slot, filled


def offset_of(table, hop):
    offset = jnp.int32(0)
    for k in range(4):
        offset = jnp.where(table[k] == hop, table[4 + k], offset)
    return offset


def home_slot(table, hop):
    slot, filled = chosen(table, hop)
    count = jnp.int32(0)
    for k in range(4):
        count = count + (table[k] != 0).astype(jnp.int32)
    for other in HOPS:
        _, other_filled = chosen(table, other)
        count = count + ((other < hop) & jnp.logical_not(other_filled)).astype(jnp.int32)
    return jnp.where(filled, slot, count), filled


def hop_of(place, stride):
    if place > 1:
        return jnp.int32(2 if place == 2 else -2)
    parity = (lax.axis_index("tm") // stride) % 2
    near = (1 - 2 * parity).astype(jnp.int32)
    return near if place == 0 else -near


def pack_kernel(places, stride, table, dual, *refs):
    count = len(places)
    outs, (held, sems) = refs[:count], refs[count:]
    depth, rows = dual.shape[1:3]
    moves = []
    for j, place in enumerate(places):
        slot, _ = chosen(table, hop_of(place, stride))
        for half in range(2):
            source = dual.at[slot, :, :, pl.ds(half * LANES, LANES)]
            moves.append(
                pltpu.make_async_copy(source, held.at[j, :, half, pl.ds(RIM, rows), :], sems.at[2 * j + half])
            )
    for m in moves:
        m.start()
    for j in range(count):
        for z in range(depth):
            for half in range(2):
                held[j, z, half, pl.ds(0, RIM), :] = jnp.zeros((RIM, LANES), jnp.float32)
                held[j, z, half, pl.ds(RIM + rows, RIM), :] = jnp.zeros((RIM, LANES), jnp.float32)
    for j, place in enumerate(places):
        offset = offset_of(table, hop_of(place, stride))
        moves[2 * j].wait()
        moves[2 * j + 1].wait()

        def body(step, carry):
            y = pl.multiple_of(step * STEP, STEP)
            for z in range(depth):
                for half in range(2):
                    outs[j][z, pl.ds(y, STEP), pl.ds(half * LANES, LANES)] = held[
                        j, z, half, pl.ds(RIM + y + offset, STEP), :
                    ]
            return carry

        lax.fori_loop(0, rows // STEP, body, 0)


def pack(places, stride, table, dual):
    _, depth, rows, columns = dual.shape
    count = len(places)
    return pl.pallas_call(
        functools.partial(pack_kernel, places, stride),
        in_specs=[pl.BlockSpec(memory_space=pltpu.SMEM), pl.BlockSpec(memory_space=pltpu.HBM)],
        out_specs=[pl.BlockSpec(memory_space=pltpu.VMEM)] * count,
        out_shape=[jax.ShapeDtypeStruct((depth, rows, columns), jnp.float32)] * count,
        scratch_shapes=[
            pltpu.VMEM((count, depth, 2, rows + 2 * RIM, LANES), jnp.float32),
            pltpu.SemaphoreType.DMA((2 * count,)),
        ],
        compiler_params=pltpu.CompilerParams(vmem_limit_bytes=8 << 20),
        cost_estimate=pl.CostEstimate(
            flops=0, bytes_accessed=2 * count * 4 * depth * rows * columns, transcendentals=0
        ),
    )(table, dual)


def box_rows(sums, z, half, start):
    return (
        sums[z, half, pl.ds(start - 1, STEP), :]
        + sums[z, half, pl.ds(start, STEP), :]
        + sums[z, half, pl.ds(start + 1, STEP), :]
    )


def box_lanes(left, right, lane):
    zero = jnp.zeros_like(left)
    left_up, right_up = pltpu.roll(left, 1, 1), pltpu.roll(right, 1, 1)
    left_down, right_down = pltpu.roll(left, LANES - 1, 1), pltpu.roll(right, LANES - 1, 1)
    first, last = lane == 0, lane == LANES - 1
    return (
        left + jnp.where(first, zero, left_up) + jnp.where(last, right_down, left_down),
        right + jnp.where(first, left_up, right_up) + jnp.where(last, zero, right_down),
    )


def pair_kernel(places, first, stride, table, *refs):
    count = len(places)
    refs = list(refs)
    take = lambda k: [refs.pop(0) for _ in range(k)]
    tables = take(count)
    image, above, below, dual, start = take(5)
    partners, tails, heads = take(count), take(count), take(count)
    if not first:
        take(1)
    fresh_out, total = take(2)
    weights, gains = take(count), take(count)
    held, own_sums, in_sums, fresh, sems, out_sems = refs
    depth, rows, _ = image.shape
    f32 = jnp.float32

    def copies(i):
        stacked = places[i][1]
        moves = []
        for half in range(2):
            lanes = pl.ds(half * LANES, LANES)
            moves.append((partners[i].at[:, :, lanes], held.at[i, pl.ds(1, depth), half, pl.ds(EDGE, rows), :]))
            moves.append((tails[i].at[stacked, :, lanes], held.at[i, 0, half, pl.ds(EDGE, rows), :]))
            moves.append((heads[i].at[stacked, :, lanes], held.at[i, depth + 1, half, pl.ds(EDGE, rows), :]))
        return [pltpu.make_async_copy(a, b, sems.at[6 * i + j]) for j, (a, b) in enumerate(moves)]

    in_copies = [copies(i) for i in range(count)]
    for group in in_copies:
        for c in group:
            c.start()
    for i in range(count):
        for z in range(depth + 2):
            for half in range(2):
                held[i, z, half, pl.ds(0, EDGE), :] = jnp.zeros((EDGE, LANES), f32)
                held[i, z, half, pl.ds(EDGE + rows, EDGE), :] = jnp.zeros((EDGE, LANES), f32)
    for z in range(depth):
        for half in range(2):
            own_sums[z, half, pl.ds(0, RIM), :] = jnp.zeros((RIM, LANES), f32)
            own_sums[z, half, pl.ds(RIM + rows, RIM), :] = jnp.zeros((RIM, LANES), f32)

    row = lax.broadcasted_iota(jnp.int32, (STEP, LANES), 0)
    lane = lax.broadcasted_iota(jnp.int32, (STEP, LANES), 1)

    def mine(z, half, y):
        here, lanes = pl.ds(pl.multiple_of(y, 8), STEP), pl.ds(half * LANES, LANES)
        if z == 0:
            return above[0, here, lanes]
        if z == depth + 1:
            return below[0, here, lanes]
        return image[z - 1, here, lanes]

    def store_sums(sums, half, y, size, squares):
        for z in range(depth):
            sums[z, half, pl.ds(pl.multiple_of(RIM + y, 8), size), :] = squares[z] + squares[z + 1] + squares[z + 2]

    out_copies = []
    for i in range(count):
        hop = hop_of(places[i][0], stride)
        source, _ = chosen(table, hop)
        own_offset = offset_of(table, hop)
        slot, filled = home_slot(table, hop)
        bound = jnp.where(filled, f32(dual_bound), f32(0.0))
        _, in_filled = chosen(tables[i], -hop)
        in_offset = offset_of(tables[i], -hop)
        low = jnp.where(in_filled, -in_offset, 4 * rows)
        high = rows - 1 - in_offset
        for c in in_copies[i]:
            c.wait()

        def theirs(z, half, y, shift, size=STEP):
            return held[i, z, half, pl.ds(EDGE + y + shift, size), :]

        for y in (-RIM, rows):
            for half in range(2):
                values = [theirs(z, half, y, in_offset, RIM) for z in range(depth + 2)]
                store_sums(in_sums, half, y, RIM, [v * v for v in values])

        def gather(step, carry):
            y = pl.multiple_of(step * STEP, STEP)
            inside = (row + y >= low) & (row + y <= high)
            for half in range(2):
                own_squares, in_squares = [], []
                for z in range(depth + 2):
                    value = mine(z, half, y)
                    own_square = theirs(z, half, y, -own_offset) - value
                    own_squares.append(own_square * own_square)
                    in_square = jnp.where(inside, value, 0.0) - theirs(z, half, y, in_offset)
                    in_squares.append(in_square * in_square)
                store_sums(own_sums, half, y, STEP, own_squares)
                store_sums(in_sums, half, y, STEP, in_squares)
            return carry

        def apply(step, carry):
            y = pl.multiple_of(step * STEP, STEP)
            inside = (row + y >= low) & (row + y <= high)
            here = pl.ds(y, STEP)
            for z in range(depth):
                own_box = box_lanes(box_rows(own_sums, z, 0, RIM + y), box_rows(own_sums, z, 1, RIM + y), lane)
                in_box = box_lanes(box_rows(in_sums, z, 0, RIM + y), box_rows(in_sums, z, 1, RIM + y), lane)
                for half in range(2):
                    lanes = pl.ds(half * LANES, LANES)
                    value = mine(z + 1, half, y)
                    weight = jnp.exp(own_box[half] * patch)
                    contrast = theirs(z + 1, half, y, -own_offset) - value
                    step_to = dual[source, z, here, lanes] + (dual_step * weight) * contrast
                    step_to = jnp.minimum(jnp.maximum(step_to, -bound), bound)
                    fresh[i, z, here, lanes] = step_to
                    flux = (weight * step_to) * flow
                    if i > 0:
                        total[z, here, lanes] = total[z, here, lanes] + flux
                    elif first:
                        total[z, here, lanes] = scale * value + (flow * fidelity) * start[z, here, lanes] + flux
                    else:
                        total[z, here, lanes] = start[z, here, lanes] + flux
                    weight = jnp.exp(in_box[half] * patch)
                    weights[i][z, here, lanes] = jnp.where(inside, weight, 0.0)
                    gains[i][z, here, lanes] = (dual_step * weight) * (value - theirs(z + 1, half, y, in_offset))
            return carry

        steps = rows // STEP
        lax.fori_loop(0, steps, gather, 0)
        for part in range(PARTS):
            lax.fori_loop(part * steps // PARTS, (part + 1) * steps // PARTS, apply, 0)
            some = pl.ds(part * rows // PARTS, rows // PARTS)
            done = pltpu.make_async_copy(
                fresh.at[i, :, some, :], fresh_out.at[slot, :, some, :], out_sems.at[PARTS * i + part]
            )
            done.start()
            out_copies.append(done)
    for c in out_copies:
        c.wait()


def pairs(places, stride, table, tables, image, above, below, dual, start, partners, tails, heads, fresh=None):
    count = len(places)
    depth, rows, columns = image.shape
    first = fresh is None
    f32 = jnp.float32
    block = jax.ShapeDtypeStruct(image.shape, f32)
    any_spec = pl.BlockSpec(memory_space=pl.ANY)
    vmem_spec = pl.BlockSpec(memory_space=pltpu.VMEM)
    smem = pl.BlockSpec(memory_space=pltpu.SMEM)
    operands = [table, *tables, image, above, below, dual, start, *partners, *tails, *heads]
    specs = [smem] * (1 + count) + [vmem_spec] * 5 + [any_spec] * (3 * count)
    aliases = {}
    if not first:
        aliases = {len(operands): 0}
        operands.append(fresh)
        specs.append(any_spec)
    cells = depth * rows * columns
    return pl.pallas_call(
        functools.partial(pair_kernel, places, first, stride),
        in_specs=specs,
        out_specs=[any_spec] + [vmem_spec] * (1 + 2 * count),
        out_shape=[jax.ShapeDtypeStruct(dual.shape, f32)] + [block] * (1 + 2 * count),
        input_output_aliases=aliases,
        scratch_shapes=[
            pltpu.VMEM((count, depth + 2, 2, rows + 2 * EDGE, LANES), f32),
            pltpu.VMEM((depth, 2, rows + 2 * RIM, LANES), f32),
            pltpu.VMEM((depth, 2, rows + 2 * RIM, LANES), f32),
            pltpu.VMEM((count, depth, rows, columns), f32),
            pltpu.SemaphoreType.DMA((6 * count,)),
            pltpu.SemaphoreType.DMA((PARTS * count,)),
        ],
        compiler_params=pltpu.CompilerParams(vmem_limit_bytes=24 << 20),
        cost_estimate=pl.CostEstimate(
            flops=count * 60 * cells, bytes_accessed=4 * (3 + 7 * count) * cells, transcendentals=2 * count * cells
        ),
    )(*operands)


def settle_kernel(count, total, *refs):
    duals, weights, gains, out = refs[:count], refs[count : 2 * count], refs[2 * count : 3 * count], refs[-1]
    depth, rows, _ = total.shape

    def body(step, carry):
        here = pl.ds(pl.multiple_of(step * STEP, STEP), STEP)
        for z in range(depth):
            arriving = None
            for i in range(count):
                value = duals[i][z, here, :] + gains[i][z, here, :]
                value = weights[i][z, here, :] * jnp.minimum(jnp.maximum(value, -dual_bound), dual_bound)
                arriving = value if arriving is None else arriving + value
            out[z, here, :] = total[z, here, :] - flow * arriving
        return carry

    lax.fori_loop(0, rows // STEP, body, 0)


def settle(total, duals, weights, gains):
    count = len(duals)
    vmem_spec = pl.BlockSpec(memory_space=pltpu.VMEM)
    return pl.pallas_call(
        functools.partial(settle_kernel, count),
        in_specs=[vmem_spec] * (1 + 3 * count),
        out_specs=vmem_spec,
        out_shape=jax.ShapeDtypeStruct(total.shape, jnp.float32),
        compiler_params=pltpu.CompilerParams(vmem_limit_bytes=20 << 20),
        cost_estimate=pl.CostEstimate(
            flops=5 * count * total.size, bytes_accessed=4 * (2 + 3 * count) * total.size, transcendentals=0
        ),
    )(total, *duals, *weights, *gains)


def shards(volume, prior_image, dual_pairs, pair_cycle, pair_offset):
    frames = lax.axis_size("tm")
    spaces = lax.axis_size("space")
    stride = frames // CYCLES
    image = volume[0]
    dual = dual_pairs[0]
    cycle_of = lambda t: t // stride
    every = range(frames)
    swap = [(t, t + stride if cycle_of(t) % 2 == 0 else t - stride) for t in every]
    cross = [(t, t - stride if cycle_of(t) % 2 == 0 else t + stride) for t in every]
    cross = [(a, b) for a, b in cross if 0 <= b < frames]
    later = [(t, t + 2 * stride) for t in every if t + 2 * stride < frames]
    sooner = [(t, t - 2 * stride) for t in every if t - 2 * stride >= 0]
    relay = [(t, t + 2 * stride if cycle_of(t) % 2 == 0 else t - 2 * stride) for t in every]
    relay = [(a, b) for a, b in relay if 0 <= b < frames]
    onward = [(s, s + 1) for s in range(spaces - 1)]
    backward = [(s + 1, s) for s in range(spaces - 1)]

    def send(x, pairs_, axis="tm"):
        return lax.ppermute(x, axis, pairs_)

    table = jnp.concatenate([pair_cycle[0], pair_offset[0]])

    near_image = send(image, swap)
    before_image = send(image, later)
    after_image = send(image, sooner)
    near_dual, far_dual = pack((0, 1), stride, table, dual)
    near_dual = send(near_dual, swap)
    far_dual = send(far_dual, cross)
    far_image = send(near_image, relay)
    near_table = send(table, swap)
    far_table = send(table, cross)
    before_table = send(table, later)
    after_table = send(table, sooner)

    stack = (image, near_image, after_image, before_image)
    bottoms = jnp.stack([x[-1] for x in stack])
    tops = jnp.stack([x[0] for x in stack])
    tails = send(bottoms, onward, "space")
    heads = send(tops, backward, "space")
    later_dual, sooner_dual = pack((2, 3), stride, table, dual)
    before_dual = send(later_dual, later)
    after_dual = send(sooner_dual, sooner)
    fresh, total, wn, wa, gn, ga = pairs(
        ((0, 1), (2, 2)), stride, table, (near_table, after_table), image, tails, heads, dual, prior_image[0],
        (near_image, after_image), (tails,) * 2, (heads,) * 2,
    )
    far_tail = send(far_image[-1:], onward, "space")
    far_head = send(far_image[:1], backward, "space")
    fresh, total, wb, wf, gb, gf = pairs(
        ((3, 3), (1, 0)), stride, table, (before_table, far_table), image, tails, heads, dual, total,
        (before_image, far_image), (tails, far_tail), (heads, far_head), fresh,
    )
    volume_next = settle(
        total, (near_dual, after_dual, before_dual, far_dual), (wn, wa, wb, wf), (gn, ga, gb, gf)
    )
    return (volume_next[None], fresh[None])


def solution(mesh):
    return jax.shard_map(
        shards,
        mesh=mesh,
        in_specs=(
            P("tm", "space", None, None),
            P("tm", "space", None, None),
            P("tm", None, "space", None, None),
            P("tm", None),
            P("tm", None),
        ),
        out_specs=(P("tm", "space", None, None), P("tm", None, "space", None, None)),
        check_vma=False,
    )
```

```python
import functools

import jax
import jax.numpy as jnp
from jax import lax
from jax.experimental import pallas as pl
from jax.experimental.pallas import tpu as pltpu
from jax.sharding import PartitionSpec as P


CYCLES = 8
HOPS = (-2, -1, 1, 2)

dual_step = 0.5
primal_step = 0.25
dual_bound = 0.3
fidelity = 1.0
scale = 1.0 / (1.0 + primal_step * fidelity)
flow = primal_step * scale
patch = -1.0 / (27.0 * 4.0)


LANES = 128
STEP = 32
PARTS = 2
EDGE = 16
RIM = 8


def chosen(table, hop):
    slot = jnp.int32(0)
    filled = table[0] == hop
    for k in range(1, 4):
        hit = table[k] == hop
        slot = jnp.where(hit, k, slot)
        filled = filled | hit
    return slot, filled


def offset_of(table, hop):
    offset = jnp.int32(0)
    for k in range(4):
        offset = jnp.where(table[k] == hop, table[4 + k], offset)
    return offset


def home_slot(table, hop):
    slot, filled = chosen(table, hop)
    count = jnp.int32(0)
    for k in range(4):
        count = count + (table[k] != 0).astype(jnp.int32)
    for other in HOPS:
        _, other_filled = chosen(table, other)
        count = count + ((other < hop) & jnp.logical_not(other_filled)).astype(jnp.int32)
    return jnp.where(filled, slot, count), filled


def hop_of(place, stride):
    width = 1 if place < 2 else 2
    parity = (lax.axis_index("tm") // (stride * width)) % 2
    near = (width * (1 - 2 * parity)).astype(jnp.int32)
    return near if place % 2 == 0 else -near


def pack_kernel(places, stride, table, dual, *refs):
    count = len(places)
    outs, (held, sems) = refs[:count], refs[count:]
    depth, rows = dual.shape[1:3]
    moves = []
    for j, place in enumerate(places):
        slot, _ = chosen(table, hop_of(place, stride))
        for half in range(2):
            source = dual.at[slot, :, :, pl.ds(half * LANES, LANES)]
            moves.append(
                pltpu.make_async_copy(source, held.at[j, :, half, pl.ds(RIM, rows), :], sems.at[2 * j + half])
            )
    for m in moves:
        m.start()
    for j in range(count):
        for z in range(depth):
            for half in range(2):
                held[j, z, half, pl.ds(0, RIM), :] = jnp.zeros((RIM, LANES), jnp.float32)
                held[j, z, half, pl.ds(RIM + rows, RIM), :] = jnp.zeros((RIM, LANES), jnp.float32)
    for j, place in enumerate(places):
        offset = offset_of(table, hop_of(place, stride))
        moves[2 * j].wait()
        moves[2 * j + 1].wait()

        def body(step, carry):
            y = pl.multiple_of(step * STEP, STEP)
            for z in range(depth):
                for half in range(2):
                    outs[j][z, pl.ds(y, STEP), pl.ds(half * LANES, LANES)] = held[
                        j, z, half, pl.ds(RIM + y + offset, STEP), :
                    ]
            return carry

        lax.fori_loop(0, rows // STEP, body, 0)


def pack(places, stride, table, dual):
    _, depth, rows, columns = dual.shape
    count = len(places)
    return pl.pallas_call(
        functools.partial(pack_kernel, places, stride),
        in_specs=[pl.BlockSpec(memory_space=pltpu.SMEM), pl.BlockSpec(memory_space=pltpu.HBM)],
        out_specs=[pl.BlockSpec(memory_space=pltpu.VMEM)] * count,
        out_shape=[jax.ShapeDtypeStruct((depth, rows, columns), jnp.float32)] * count,
        scratch_shapes=[
            pltpu.VMEM((count, depth, 2, rows + 2 * RIM, LANES), jnp.float32),
            pltpu.SemaphoreType.DMA((2 * count,)),
        ],
        compiler_params=pltpu.CompilerParams(vmem_limit_bytes=8 << 20),
        cost_estimate=pl.CostEstimate(
            flops=0, bytes_accessed=2 * count * 4 * depth * rows * columns, transcendentals=0
        ),
    )(table, pltpu.with_memory_space_constraint(dual, pltpu.HBM))


def box_rows(sums, z, half, start):
    return (
        sums[z, half, pl.ds(start - 1, STEP), :]
        + sums[z, half, pl.ds(start, STEP), :]
        + sums[z, half, pl.ds(start + 1, STEP), :]
    )


def box_lanes(left, right, lane):
    zero = jnp.zeros_like(left)
    left_up, right_up = pltpu.roll(left, 1, 1), pltpu.roll(right, 1, 1)
    left_down, right_down = pltpu.roll(left, LANES - 1, 1), pltpu.roll(right, LANES - 1, 1)
    first, last = lane == 0, lane == LANES - 1
    return (
        left + jnp.where(first, zero, left_up) + jnp.where(last, right_down, left_down),
        right + jnp.where(first, left_up, right_up) + jnp.where(last, zero, right_down),
    )


def pair_kernel(places, first, stride, table, *refs):
    count = len(places)
    refs = list(refs)
    take = lambda k: [refs.pop(0) for _ in range(k)]
    tables = take(count)
    image, dual, start = take(3)
    partners, inner, outer, own_halos = take(count), take(count), take(count), take(2)
    if not first:
        take(1)
    fresh_out, total = take(2)
    weights, gains = take(count), take(count)
    held, rim, own_sums, in_sums, fresh, sems, out_sems = refs
    depth, rows, _ = image.shape
    f32 = jnp.float32

    even = lax.axis_index("space") % 2 == 0

    def copies(i, upper, lower):
        stacked = places[i][1]
        moves = []
        for half in range(2):
            lanes = pl.ds(half * LANES, LANES)
            moves.append((partners[i].at[:, :, lanes], held.at[i, pl.ds(1, depth), half, pl.ds(EDGE, rows), :]))
            moves.append((upper.at[stacked, :, lanes], held.at[i, 0, half, pl.ds(EDGE, rows), :]))
            moves.append((lower.at[stacked, :, lanes], held.at[i, depth + 1, half, pl.ds(EDGE, rows), :]))
        return [pltpu.make_async_copy(a, b, sems.at[6 * i + j]) for j, (a, b) in enumerate(moves)]

    def start_all(uppers, lowers, own_upper, own_lower):
        for c in rim_copies(own_upper, own_lower):
            c.start()
        for i in range(count):
            for c in copies(i, uppers[i], lowers[i]):
                c.start()

    def rim_copies(upper, lower):
        return [
            pltpu.make_async_copy(upper.at[0], rim.at[0], sems.at[6 * count]),
            pltpu.make_async_copy(lower.at[0], rim.at[1], sems.at[6 * count + 1]),
        ]

    pl.when(even)(lambda: start_all(outer, inner, own_halos[1], own_halos[0]))
    pl.when(jnp.logical_not(even))(lambda: start_all(inner, outer, own_halos[0], own_halos[1]))
    in_copies = [copies(i, inner[i], outer[i]) for i in range(count)]
    for i in range(count):
        for z in range(depth + 2):
            for half in range(2):
                held[i, z, half, pl.ds(0, EDGE), :] = jnp.zeros((EDGE, LANES), f32)
                held[i, z, half, pl.ds(EDGE + rows, EDGE), :] = jnp.zeros((EDGE, LANES), f32)
    for z in range(depth):
        for half in range(2):
            own_sums[z, half, pl.ds(0, RIM), :] = jnp.zeros((RIM, LANES), f32)
            own_sums[z, half, pl.ds(RIM + rows, RIM), :] = jnp.zeros((RIM, LANES), f32)

    row = lax.broadcasted_iota(jnp.int32, (STEP, LANES), 0)
    lane = lax.broadcasted_iota(jnp.int32, (STEP, LANES), 1)

    def mine(z, half, y):
        here, lanes = pl.ds(pl.multiple_of(y, 8), STEP), pl.ds(half * LANES, LANES)
        if z == 0:
            return rim[0, here, lanes]
        if z == depth + 1:
            return rim[1, here, lanes]
        return image[z - 1, here, lanes]

    def store_sums(sums, half, y, size, squares):
        for z in range(depth):
            sums[z, half, pl.ds(pl.multiple_of(RIM + y, 8), size), :] = squares[z] + squares[z + 1] + squares[z + 2]

    for c in rim_copies(*own_halos):
        c.wait()
    out_copies = []
    for i in range(count):
        hop = hop_of(places[i][0], stride)
        source, _ = chosen(table, hop)
        own_offset = offset_of(table, hop)
        slot, filled = home_slot(table, hop)
        bound = jnp.where(filled, f32(dual_bound), f32(0.0))
        _, in_filled = chosen(tables[i], -hop)
        in_offset = offset_of(tables[i], -hop)
        low = jnp.where(in_filled, -in_offset, 4 * rows)
        high = rows - 1 - in_offset
        for c in in_copies[i]:
            c.wait()

        def theirs(z, half, y, shift, size=STEP):
            return held[i, z, half, pl.ds(EDGE + y + shift, size), :]

        for y in (-RIM, rows):
            for half in range(2):
                values = [theirs(z, half, y, in_offset, RIM) for z in range(depth + 2)]
                store_sums(in_sums, half, y, RIM, [v * v for v in values])

        def gather(step, carry):
            y = pl.multiple_of(step * STEP, STEP)
            inside = (row + y >= low) & (row + y <= high)
            for half in range(2):
                own_squares, in_squares = [], []
                for z in range(depth + 2):
                    value = mine(z, half, y)
                    own_square = theirs(z, half, y, -own_offset) - value
                    own_squares.append(own_square * own_square)
                    in_square = jnp.where(inside, value, 0.0) - theirs(z, half, y, in_offset)
                    in_squares.append(in_square * in_square)
                store_sums(own_sums, half, y, STEP, own_squares)
                store_sums(in_sums, half, y, STEP, in_squares)
            return carry

        def apply(step, carry):
            y = pl.multiple_of(step * STEP, STEP)
            inside = (row + y >= low) & (row + y <= high)
            here = pl.ds(y, STEP)
            for z in range(depth):
                own_box = box_lanes(box_rows(own_sums, z, 0, RIM + y), box_rows(own_sums, z, 1, RIM + y), lane)
                in_box = box_lanes(box_rows(in_sums, z, 0, RIM + y), box_rows(in_sums, z, 1, RIM + y), lane)
                for half in range(2):
                    lanes = pl.ds(half * LANES, LANES)
                    value = mine(z + 1, half, y)
                    weight = jnp.exp(own_box[half] * patch)
                    contrast = theirs(z + 1, half, y, -own_offset) - value
                    step_to = dual[source, z, here, lanes] + (dual_step * weight) * contrast
                    step_to = jnp.minimum(jnp.maximum(step_to, -bound), bound)
                    fresh[i, z, here, lanes] = step_to
                    flux = (weight * step_to) * flow
                    if i > 0:
                        total[z, here, lanes] = total[z, here, lanes] + flux
                    elif first:
                        total[z, here, lanes] = scale * value + (flow * fidelity) * start[z, here, lanes] + flux
                    else:
                        total[z, here, lanes] = start[z, here, lanes] + flux
                    weight = jnp.exp(in_box[half] * patch)
                    weights[i][z, here, lanes] = jnp.where(inside, weight, 0.0)
                    gains[i][z, here, lanes] = (dual_step * weight) * (value - theirs(z + 1, half, y, in_offset))
            return carry

        steps = rows // STEP
        lax.fori_loop(0, steps, gather, 0)
        for part in range(PARTS):
            lax.fori_loop(part * steps // PARTS, (part + 1) * steps // PARTS, apply, 0)
            some = pl.ds(part * rows // PARTS, rows // PARTS)
            done = pltpu.make_async_copy(
                fresh.at[i, :, some, :], fresh_out.at[slot, :, some, :], out_sems.at[PARTS * i + part]
            )
            done.start()
            out_copies.append(done)
    for c in out_copies:
        c.wait()


def pairs(places, stride, table, tables, image, dual, start, partners, inner, outer, own_halos, fresh=None):
    count = len(places)
    depth, rows, columns = image.shape
    first = fresh is None
    f32 = jnp.float32
    block = jax.ShapeDtypeStruct(image.shape, f32)
    any_spec = pl.BlockSpec(memory_space=pl.ANY)
    vmem_spec = pl.BlockSpec(memory_space=pltpu.VMEM)
    smem = pl.BlockSpec(memory_space=pltpu.SMEM)
    operands = [table, *tables, image, dual, start, *partners, *inner, *outer, *own_halos]
    specs = [smem] * (1 + count) + [vmem_spec] * 3 + [any_spec] * (3 * count + 2)
    aliases = {}
    if not first:
        aliases = {len(operands): 0}
        operands.append(fresh)
        specs.append(any_spec)
    cells = depth * rows * columns
    return pl.pallas_call(
        functools.partial(pair_kernel, places, first, stride),
        in_specs=specs,
        out_specs=[any_spec] + [vmem_spec] * (1 + 2 * count),
        out_shape=[jax.ShapeDtypeStruct(dual.shape, f32)] + [block] * (1 + 2 * count),
        input_output_aliases=aliases,
        scratch_shapes=[
            pltpu.VMEM((count, depth + 2, 2, rows + 2 * EDGE, LANES), f32),
            pltpu.VMEM((2, rows, columns), f32),
            pltpu.VMEM((depth, 2, rows + 2 * RIM, LANES), f32),
            pltpu.VMEM((depth, 2, rows + 2 * RIM, LANES), f32),
            pltpu.VMEM((count, depth, rows, columns), f32),
            pltpu.SemaphoreType.DMA((6 * count + 2,)),
            pltpu.SemaphoreType.DMA((PARTS * count,)),
        ],
        compiler_params=pltpu.CompilerParams(vmem_limit_bytes=16 << 20),
        cost_estimate=pl.CostEstimate(
            flops=count * 60 * cells, bytes_accessed=4 * (3 + 7 * count) * cells, transcendentals=2 * count * cells
        ),
    )(*operands)


def cut_kernel(*refs):
    count = len(refs) - 3
    images, (within, across, sems) = refs[:count], refs[count:]
    last = images[0].shape[0] - 1
    even = lax.axis_index("space") % 2 == 0

    def copies(inner, outer):
        moves = []
        for k, image in enumerate(images):
            moves.append(pltpu.make_async_copy(image.at[inner], within.at[k], sems.at[2 * k]))
            moves.append(pltpu.make_async_copy(image.at[outer], across.at[k], sems.at[2 * k + 1]))
        return moves

    pl.when(even)(lambda: [c.start() for c in copies(last, 0)] and None)
    pl.when(jnp.logical_not(even))(lambda: [c.start() for c in copies(0, last)] and None)
    for c in copies(last, 0):
        c.wait()


def cut(images):
    count = len(images)
    block = (count,) + images[0].shape[1:]
    return pl.pallas_call(
        cut_kernel,
        in_specs=[pl.BlockSpec(memory_space=pl.ANY)] * count,
        out_specs=[pl.BlockSpec(memory_space=pltpu.VMEM)] * 2,
        out_shape=[jax.ShapeDtypeStruct(block, jnp.float32)] * 2,
        scratch_shapes=[pltpu.SemaphoreType.DMA((2 * count,))],
        compiler_params=pltpu.CompilerParams(vmem_limit_bytes=6 << 20),
        cost_estimate=pl.CostEstimate(flops=0, bytes_accessed=16 * count * block[1] * block[2], transcendentals=0),
    )(*images)


def settle_kernel(count, total, *refs):
    duals, weights, gains, out = refs[:count], refs[count : 2 * count], refs[2 * count : 3 * count], refs[-1]
    depth, rows, _ = total.shape

    def body(step, carry):
        here = pl.ds(pl.multiple_of(step * STEP, STEP), STEP)
        for z in range(depth):
            arriving = None
            for i in range(count):
                value = duals[i][z, here, :] + gains[i][z, here, :]
                value = weights[i][z, here, :] * jnp.minimum(jnp.maximum(value, -dual_bound), dual_bound)
                arriving = value if arriving is None else arriving + value
            out[z, here, :] = total[z, here, :] - flow * arriving
        return carry

    lax.fori_loop(0, rows // STEP, body, 0)


def settle(total, duals, weights, gains):
    count = len(duals)
    vmem_spec = pl.BlockSpec(memory_space=pltpu.VMEM)
    return pl.pallas_call(
        functools.partial(settle_kernel, count),
        in_specs=[vmem_spec] * (1 + 3 * count),
        out_specs=vmem_spec,
        out_shape=jax.ShapeDtypeStruct(total.shape, jnp.float32),
        compiler_params=pltpu.CompilerParams(vmem_limit_bytes=10 << 20),
        cost_estimate=pl.CostEstimate(
            flops=5 * count * total.size, bytes_accessed=4 * (2 + 3 * count) * total.size, transcendentals=0
        ),
    )(total, *duals, *weights, *gains)


def shards(volume, prior_image, dual_pairs, pair_cycle, pair_offset):
    frames = lax.axis_size("tm")
    spaces = lax.axis_size("space")
    stride = frames // CYCLES
    image = volume[0]
    dual = dual_pairs[0]
    cycle_of = lambda t: t // stride
    every = range(frames)
    swap = [(t, t + stride if cycle_of(t) % 2 == 0 else t - stride) for t in every]
    cross = [(t, t - stride if cycle_of(t) % 2 == 0 else t + stride) for t in every]
    cross = [(a, b) for a, b in cross if 0 <= b < frames]
    wide_swap = [(t, t + 2 * stride if cycle_of(t) // 2 % 2 == 0 else t - 2 * stride) for t in every]
    wide_cross = [(t, t - 2 * stride if cycle_of(t) // 2 % 2 == 0 else t + 2 * stride) for t in every]
    wide_cross = [(a, b) for a, b in wide_cross if 0 <= b < frames]
    relay = [(t, t + 2 * stride if cycle_of(t) % 2 == 0 else t - 2 * stride) for t in every]
    relay = [(a, b) for a, b in relay if 0 <= b < frames]
    inner = [(s, s ^ 1) for s in range(spaces)]
    outer = [(s, s - 1 if s % 2 == 0 else s + 1) for s in range(spaces)]
    outer = [(a, b) for a, b in outer if 0 <= b < spaces]

    def send(x, pairs_, axis="tm"):
        return lax.ppermute(x, axis, pairs_)

    table = jnp.concatenate([pair_cycle[0], pair_offset[0]])

    def halos(images):
        within, across = cut(images)
        return send(within, inner, "space"), send(across, outer, "space")

    near_image = send(image, swap)
    wide_near_image = send(image, wide_swap)
    wide_far_image = send(image, wide_cross)
    near_table = send(table, swap)
    far_table = send(table, cross)
    wide_near_table = send(table, wide_swap)
    wide_far_table = send(table, wide_cross)
    near_dual, far_dual = pack((0, 1), stride, table, dual)
    near_dual = send(near_dual, swap)
    far_dual = send(far_dual, cross)
    far_image = send(near_image, relay)

    within, across = halos((image, near_image, wide_near_image, wide_far_image))
    wide_near_dual, wide_far_dual = pack((2, 3), stride, table, dual)
    wide_near_dual = send(wide_near_dual, wide_swap)
    wide_far_dual = send(wide_far_dual, wide_cross)
    fresh, total, w0, w2, g0, g2 = pairs(
        ((0, 1), (2, 2)), stride, table, (near_table, wide_near_table), image, dual, prior_image[0],
        (near_image, wide_near_image), (within,) * 2, (across,) * 2, (within, across),
    )
    far_within, far_across = halos((far_image,))
    fresh, total, w3, w1, g3, g1 = pairs(
        ((3, 3), (1, 0)), stride, table, (wide_far_table, far_table), image, dual, total,
        (wide_far_image, far_image), (within, far_within), (across, far_across), (within, across), fresh,
    )
    volume_next = settle(
        total, (near_dual, wide_near_dual, wide_far_dual, far_dual), (w0, w2, w3, w1), (g0, g2, g3, g1)
    )
    return (volume_next[None], fresh[None])


def solution(mesh):
    return jax.shard_map(
        shards,
        mesh=mesh,
        in_specs=(
            P("tm", "space", None, None),
            P("tm", "space", None, None),
            P("tm", None, "space", None, None),
            P("tm", None),
            P("tm", None),
        ),
        out_specs=(P("tm", "space", None, None), P("tm", None, "space", None, None)),
        check_vma=False,
    )
```

```python
import functools

import jax
import jax.numpy as jnp
from jax import lax
from jax.experimental import pallas as pl
from jax.experimental.pallas import tpu as pltpu
from jax.sharding import PartitionSpec as P


CYCLES = 8
HOPS = (-2, -1, 1, 2)

dual_step = 0.5
primal_step = 0.25
dual_bound = 0.3
fidelity = 1.0
scale = 1.0 / (1.0 + primal_step * fidelity)
flow = primal_step * scale
patch = -1.0 / (27.0 * 4.0)


LANES = 128
STEP = 32
PARTS = 2
EDGE = 16
RIM = 8


def chosen(table, hop):
    slot = jnp.int32(0)
    filled = table[0] == hop
    for k in range(1, 4):
        hit = table[k] == hop
        slot = jnp.where(hit, k, slot)
        filled = filled | hit
    return slot, filled


def offset_of(table, hop):
    offset = jnp.int32(0)
    for k in range(4):
        offset = jnp.where(table[k] == hop, table[4 + k], offset)
    return offset


def home_slot(table, hop):
    slot, filled = chosen(table, hop)
    count = jnp.int32(0)
    for k in range(4):
        count = count + (table[k] != 0).astype(jnp.int32)
    for other in HOPS:
        _, other_filled = chosen(table, other)
        count = count + ((other < hop) & jnp.logical_not(other_filled)).astype(jnp.int32)
    return jnp.where(filled, slot, count), filled


def hop_of(place, stride):
    width = 1 if place < 2 else 2
    parity = (lax.axis_index("tm") // (stride * width)) % 2
    near = (width * (1 - 2 * parity)).astype(jnp.int32)
    return near if place % 2 == 0 else -near


def piece_of(pieces, z):
    for piece, size in enumerate(pieces):
        if z < size:
            return piece, z
        z -= size


def pack_kernel(places, pieces, stride, table, dual, *refs):
    count = len(places)
    outs, (held, sems) = refs[: count * len(pieces)], refs[count * len(pieces) :]
    depth, rows = dual.shape[1:3]
    moves = []
    for j, place in enumerate(places):
        slot, _ = chosen(table, hop_of(place, stride))
        for half in range(2):
            source = dual.at[slot, :, :, pl.ds(half * LANES, LANES)]
            moves.append(
                pltpu.make_async_copy(source, held.at[j, :, half, pl.ds(RIM, rows), :], sems.at[2 * j + half])
            )
    for m in moves:
        m.start()
    for j in range(count):
        for z in range(depth):
            for half in range(2):
                held[j, z, half, pl.ds(0, RIM), :] = jnp.zeros((RIM, LANES), jnp.float32)
                held[j, z, half, pl.ds(RIM + rows, RIM), :] = jnp.zeros((RIM, LANES), jnp.float32)
    for j, place in enumerate(places):
        offset = offset_of(table, hop_of(place, stride))
        moves[2 * j].wait()
        moves[2 * j + 1].wait()

        def body(step, carry):
            y = pl.multiple_of(step * STEP, STEP)
            for z in range(depth):
                for half in range(2):
                    piece, within = piece_of(pieces, z)
                    outs[j * len(pieces) + piece][within, pl.ds(y, STEP), pl.ds(half * LANES, LANES)] = held[
                        j, z, half, pl.ds(RIM + y + offset, STEP), :
                    ]
            return carry

        lax.fori_loop(0, rows // STEP, body, 0)


def pack(places, pieces, stride, table, dual):
    _, depth, rows, columns = dual.shape
    count = len(places)
    return pl.pallas_call(
        functools.partial(pack_kernel, places, pieces, stride),
        in_specs=[pl.BlockSpec(memory_space=pltpu.SMEM), pl.BlockSpec(memory_space=pltpu.HBM)],
        out_specs=[pl.BlockSpec(memory_space=pltpu.VMEM)] * (count * len(pieces)),
        out_shape=[jax.ShapeDtypeStruct((size, rows, columns), jnp.float32) for size in pieces] * count,
        scratch_shapes=[
            pltpu.VMEM((count, depth, 2, rows + 2 * RIM, LANES), jnp.float32),
            pltpu.SemaphoreType.DMA((2 * count,)),
        ],
        compiler_params=pltpu.CompilerParams(vmem_limit_bytes=8 << 20),
        cost_estimate=pl.CostEstimate(
            flops=0, bytes_accessed=2 * count * 4 * depth * rows * columns, transcendentals=0
        ),
    )(table, pltpu.with_memory_space_constraint(dual, pltpu.HBM))


def box_rows(sums, z, half, start):
    return (
        sums[z, half, pl.ds(start - 1, STEP), :]
        + sums[z, half, pl.ds(start, STEP), :]
        + sums[z, half, pl.ds(start + 1, STEP), :]
    )


def box_lanes(left, right, lane):
    zero = jnp.zeros_like(left)
    left_up, right_up = pltpu.roll(left, 1, 1), pltpu.roll(right, 1, 1)
    left_down, right_down = pltpu.roll(left, LANES - 1, 1), pltpu.roll(right, LANES - 1, 1)
    first, last = lane == 0, lane == LANES - 1
    return (
        left + jnp.where(first, zero, left_up) + jnp.where(last, right_down, left_down),
        right + jnp.where(first, left_up, right_up) + jnp.where(last, zero, right_down),
    )


def pair_kernel(places, first, stride, table, *refs):
    count = len(places)
    refs = list(refs)
    take = lambda k: [refs.pop(0) for _ in range(k)]
    tables = take(count)
    image, dual, start = take(3)
    partners, inner, outer, own_halos = take(count), take(count), take(count), take(2)
    if not first:
        take(1)
    fresh_out, total = take(2)
    weights, gains = take(count), take(count)
    held, rim, own_sums, in_sums, fresh, sems, out_sems = refs
    depth, rows, _ = image.shape
    f32 = jnp.float32

    even = lax.axis_index("space") % 2 == 0

    def copies(i, upper, lower):
        stacked = places[i][1]
        moves = []
        for half in range(2):
            lanes = pl.ds(half * LANES, LANES)
            moves.append((partners[i].at[:, :, lanes], held.at[i, pl.ds(1, depth), half, pl.ds(EDGE, rows), :]))
            moves.append((upper.at[stacked, :, lanes], held.at[i, 0, half, pl.ds(EDGE, rows), :]))
            moves.append((lower.at[stacked, :, lanes], held.at[i, depth + 1, half, pl.ds(EDGE, rows), :]))
        return [pltpu.make_async_copy(a, b, sems.at[6 * i + j]) for j, (a, b) in enumerate(moves)]

    def start_all(uppers, lowers, own_upper, own_lower):
        for c in rim_copies(own_upper, own_lower):
            c.start()
        for i in range(count):
            for c in copies(i, uppers[i], lowers[i]):
                c.start()

    def rim_copies(upper, lower):
        return [
            pltpu.make_async_copy(upper.at[0], rim.at[0], sems.at[6 * count]),
            pltpu.make_async_copy(lower.at[0], rim.at[1], sems.at[6 * count + 1]),
        ]

    pl.when(even)(lambda: start_all(outer, inner, own_halos[1], own_halos[0]))
    pl.when(jnp.logical_not(even))(lambda: start_all(inner, outer, own_halos[0], own_halos[1]))
    in_copies = [copies(i, inner[i], outer[i]) for i in range(count)]
    for i in range(count):
        for z in range(depth + 2):
            for half in range(2):
                held[i, z, half, pl.ds(0, EDGE), :] = jnp.zeros((EDGE, LANES), f32)
                held[i, z, half, pl.ds(EDGE + rows, EDGE), :] = jnp.zeros((EDGE, LANES), f32)
    for z in range(depth):
        for half in range(2):
            own_sums[z, half, pl.ds(0, RIM), :] = jnp.zeros((RIM, LANES), f32)
            own_sums[z, half, pl.ds(RIM + rows, RIM), :] = jnp.zeros((RIM, LANES), f32)

    row = lax.broadcasted_iota(jnp.int32, (STEP, LANES), 0)
    lane = lax.broadcasted_iota(jnp.int32, (STEP, LANES), 1)

    def mine(z, half, y):
        here, lanes = pl.ds(pl.multiple_of(y, 8), STEP), pl.ds(half * LANES, LANES)
        if z == 0:
            return rim[0, here, lanes]
        if z == depth + 1:
            return rim[1, here, lanes]
        return image[z - 1, here, lanes]

    def store_sums(sums, half, y, size, squares):
        for z in range(depth):
            sums[z, half, pl.ds(pl.multiple_of(RIM + y, 8), size), :] = squares[z] + squares[z + 1] + squares[z + 2]

    for c in rim_copies(*own_halos):
        c.wait()
    out_copies = []
    for i in range(count):
        hop = hop_of(places[i][0], stride)
        source, _ = chosen(table, hop)
        own_offset = offset_of(table, hop)
        slot, filled = home_slot(table, hop)
        bound = jnp.where(filled, f32(dual_bound), f32(0.0))
        _, in_filled = chosen(tables[i], -hop)
        in_offset = offset_of(tables[i], -hop)
        low = jnp.where(in_filled, -in_offset, 4 * rows)
        high = rows - 1 - in_offset
        for c in in_copies[i]:
            c.wait()

        def theirs(z, half, y, shift, size=STEP):
            return held[i, z, half, pl.ds(EDGE + y + shift, size), :]

        for y in (-RIM, rows):
            for half in range(2):
                values = [theirs(z, half, y, in_offset, RIM) for z in range(depth + 2)]
                store_sums(in_sums, half, y, RIM, [v * v for v in values])

        def gather(step, carry):
            y = pl.multiple_of(step * STEP, STEP)
            inside = (row + y >= low) & (row + y <= high)
            for half in range(2):
                own_squares, in_squares = [], []
                for z in range(depth + 2):
                    value = mine(z, half, y)
                    own_square = theirs(z, half, y, -own_offset) - value
                    own_squares.append(own_square * own_square)
                    in_square = jnp.where(inside, value, 0.0) - theirs(z, half, y, in_offset)
                    in_squares.append(in_square * in_square)
                store_sums(own_sums, half, y, STEP, own_squares)
                store_sums(in_sums, half, y, STEP, in_squares)
            return carry

        def apply(step, carry):
            y = pl.multiple_of(step * STEP, STEP)
            inside = (row + y >= low) & (row + y <= high)
            here = pl.ds(y, STEP)
            for z in range(depth):
                own_box = box_lanes(box_rows(own_sums, z, 0, RIM + y), box_rows(own_sums, z, 1, RIM + y), lane)
                in_box = box_lanes(box_rows(in_sums, z, 0, RIM + y), box_rows(in_sums, z, 1, RIM + y), lane)
                for half in range(2):
                    lanes = pl.ds(half * LANES, LANES)
                    value = mine(z + 1, half, y)
                    weight = jnp.exp(own_box[half] * patch)
                    contrast = theirs(z + 1, half, y, -own_offset) - value
                    step_to = dual[source, z, here, lanes] + (dual_step * weight) * contrast
                    step_to = jnp.minimum(jnp.maximum(step_to, -bound), bound)
                    fresh[i, z, here, lanes] = step_to
                    flux = (weight * step_to) * flow
                    if i > 0:
                        total[z, here, lanes] = total[z, here, lanes] + flux
                    elif first:
                        total[z, here, lanes] = scale * value + (flow * fidelity) * start[z, here, lanes] + flux
                    else:
                        total[z, here, lanes] = start[z, here, lanes] + flux
                    weight = jnp.exp(in_box[half] * patch)
                    weights[i][z, here, lanes] = jnp.where(inside, weight, 0.0)
                    gains[i][z, here, lanes] = (dual_step * weight) * (value - theirs(z + 1, half, y, in_offset))
            return carry

        steps = rows // STEP
        lax.fori_loop(0, steps, gather, 0)
        for part in range(PARTS):
            lax.fori_loop(part * steps // PARTS, (part + 1) * steps // PARTS, apply, 0)
            some = pl.ds(part * rows // PARTS, rows // PARTS)
            done = pltpu.make_async_copy(
                fresh.at[i, :, some, :], fresh_out.at[slot, :, some, :], out_sems.at[PARTS * i + part]
            )
            done.start()
            out_copies.append(done)
    for c in out_copies:
        c.wait()


def pairs(places, stride, table, tables, image, dual, start, partners, inner, outer, own_halos, fresh=None):
    count = len(places)
    depth, rows, columns = image.shape
    first = fresh is None
    f32 = jnp.float32
    block = jax.ShapeDtypeStruct(image.shape, f32)
    any_spec = pl.BlockSpec(memory_space=pl.ANY)
    vmem_spec = pl.BlockSpec(memory_space=pltpu.VMEM)
    smem = pl.BlockSpec(memory_space=pltpu.SMEM)
    operands = [table, *tables, image, dual, start, *partners, *inner, *outer, *own_halos]
    specs = [smem] * (1 + count) + [vmem_spec] * 3 + [any_spec] * (3 * count + 2)
    aliases = {}
    if not first:
        aliases = {len(operands): 0}
        operands.append(fresh)
        specs.append(any_spec)
    cells = depth * rows * columns
    return pl.pallas_call(
        functools.partial(pair_kernel, places, first, stride),
        in_specs=specs,
        out_specs=[any_spec] + [vmem_spec] * (1 + 2 * count),
        out_shape=[jax.ShapeDtypeStruct(dual.shape, f32)] + [block] * (1 + 2 * count),
        input_output_aliases=aliases,
        scratch_shapes=[
            pltpu.VMEM((count, depth + 2, 2, rows + 2 * EDGE, LANES), f32),
            pltpu.VMEM((2, rows, columns), f32),
            pltpu.VMEM((depth, 2, rows + 2 * RIM, LANES), f32),
            pltpu.VMEM((depth, 2, rows + 2 * RIM, LANES), f32),
            pltpu.VMEM((count, depth, rows, columns), f32),
            pltpu.SemaphoreType.DMA((6 * count + 2,)),
            pltpu.SemaphoreType.DMA((PARTS * count,)),
        ],
        compiler_params=pltpu.CompilerParams(vmem_limit_bytes=20 << 20),
        cost_estimate=pl.CostEstimate(
            flops=count * 60 * cells, bytes_accessed=4 * (3 + 7 * count) * cells, transcendentals=2 * count * cells
        ),
    )(*operands)


def cut_kernel(*refs):
    count = len(refs) - 3
    images, (within, across, sems) = refs[:count], refs[count:]
    last = images[0].shape[0] - 1
    even = lax.axis_index("space") % 2 == 0

    def copies(inner, outer):
        moves = []
        for k, image in enumerate(images):
            moves.append(pltpu.make_async_copy(image.at[inner], within.at[k], sems.at[2 * k]))
            moves.append(pltpu.make_async_copy(image.at[outer], across.at[k], sems.at[2 * k + 1]))
        return moves

    pl.when(even)(lambda: [c.start() for c in copies(last, 0)] and None)
    pl.when(jnp.logical_not(even))(lambda: [c.start() for c in copies(0, last)] and None)
    for c in copies(last, 0):
        c.wait()


def cut(images):
    count = len(images)
    block = (count,) + images[0].shape[1:]
    return pl.pallas_call(
        cut_kernel,
        in_specs=[pl.BlockSpec(memory_space=pl.ANY)] * count,
        out_specs=[pl.BlockSpec(memory_space=pltpu.VMEM)] * 2,
        out_shape=[jax.ShapeDtypeStruct(block, jnp.float32)] * 2,
        scratch_shapes=[pltpu.SemaphoreType.DMA((2 * count,))],
        compiler_params=pltpu.CompilerParams(vmem_limit_bytes=6 << 20),
        cost_estimate=pl.CostEstimate(flops=0, bytes_accessed=16 * count * block[1] * block[2], transcendentals=0),
    )(*images)


def settle_kernel(count, pieces, last, total, *refs):
    refs = list(refs)
    take = lambda k: [refs.pop(0) for _ in range(k)]
    duals, weights, gains = take(count * len(pieces)), take(count), take(count)
    if last:
        result, out, sems = refs
    else:
        (out,) = refs
    depth, rows, _ = total.shape
    moves = []
    for z in range(depth):
        piece, within = piece_of(pieces, z)

        def body(step, carry):
            here = pl.ds(pl.multiple_of(step * STEP, STEP), STEP)
            arriving = None
            for i in range(count):
                value = duals[i * len(pieces) + piece][within, here, :] + gains[i][z, here, :]
                value = weights[i][z, here, :] * jnp.minimum(jnp.maximum(value, -dual_bound), dual_bound)
                arriving = value if arriving is None else arriving + value
            out[z, here, :] = total[z, here, :] - flow * arriving
            return carry

        lax.fori_loop(0, rows // STEP, body, 0)
        if last:
            moves.append(pltpu.make_async_copy(out.at[z], result.at[z], sems.at[z]))
            moves[-1].start()
    for m in moves:
        m.wait()


def settle(total, duals, pieces, weights, gains, last):
    count = len(weights)
    depth = total.shape[0]
    vmem_spec = pl.BlockSpec(memory_space=pltpu.VMEM)
    return pl.pallas_call(
        functools.partial(settle_kernel, count, pieces, last),
        in_specs=[vmem_spec] * (1 + len(duals) + 2 * count),
        out_specs=pl.BlockSpec(memory_space=pl.ANY) if last else vmem_spec,
        out_shape=jax.ShapeDtypeStruct(total.shape, jnp.float32),
        scratch_shapes=[pltpu.VMEM(total.shape, jnp.float32), pltpu.SemaphoreType.DMA((depth,))] if last else [],
        compiler_params=pltpu.CompilerParams(vmem_limit_bytes=10 << 20),
        cost_estimate=pl.CostEstimate(
            flops=5 * count * total.size, bytes_accessed=4 * (2 + 3 * count) * total.size, transcendentals=0
        ),
    )(total, *duals, *weights, *gains)


def shards(volume, prior_image, dual_pairs, pair_cycle, pair_offset):
    frames = lax.axis_size("tm")
    spaces = lax.axis_size("space")
    stride = frames // CYCLES
    image = volume[0]
    dual = dual_pairs[0]
    cycle_of = lambda t: t // stride
    every = range(frames)
    swap = [(t, t + stride if cycle_of(t) % 2 == 0 else t - stride) for t in every]
    cross = [(t, t - stride if cycle_of(t) % 2 == 0 else t + stride) for t in every]
    cross = [(a, b) for a, b in cross if 0 <= b < frames]
    wide_swap = [(t, t + 2 * stride if cycle_of(t) // 2 % 2 == 0 else t - 2 * stride) for t in every]
    wide_cross = [(t, t - 2 * stride if cycle_of(t) // 2 % 2 == 0 else t + 2 * stride) for t in every]
    wide_cross = [(a, b) for a, b in wide_cross if 0 <= b < frames]
    relay = [(t, t + 2 * stride if cycle_of(t) % 2 == 0 else t - 2 * stride) for t in every]
    relay = [(a, b) for a, b in relay if 0 <= b < frames]
    inner = [(s, s ^ 1) for s in range(spaces)]
    outer = [(s, s - 1 if s % 2 == 0 else s + 1) for s in range(spaces)]
    outer = [(a, b) for a, b in outer if 0 <= b < spaces]

    def send(x, pairs_, axis="tm"):
        return lax.ppermute(x, axis, pairs_)

    table = jnp.concatenate([pair_cycle[0], pair_offset[0]])

    def halos(images):
        within, across = cut(images)
        return send(within, inner, "space"), send(across, outer, "space")

    near_image = send(image, swap)
    wide_near_image = send(image, wide_swap)
    wide_far_image = send(image, wide_cross)
    near_table = send(table, swap)
    far_table = send(table, cross)
    wide_near_table = send(table, wide_swap)
    wide_far_table = send(table, wide_cross)
    depth = image.shape[0]
    lead = max(depth // 4, 1)
    pieces = (lead, depth - lead)
    near_dual, far_dual = pack((0, 1), (depth,), stride, table, dual)
    near_dual = send(near_dual, swap)
    far_dual = send(far_dual, cross)
    wide = list(pack((2, 3), pieces, stride, table, dual))
    wide[0] = send(wide[0], wide_swap)
    wide[2] = send(wide[2], wide_cross)
    far_image = send(near_image, relay)

    within, across = halos((image, near_image, wide_near_image, wide_far_image))
    wide[1] = send(wide[1], wide_swap)
    wide[3] = send(wide[3], wide_cross)
    fresh, total, w0, w2, w3, g0, g2, g3 = pairs(
        ((0, 1), (2, 2), (3, 3)), stride, table, (near_table, wide_near_table, wide_far_table),
        image, dual, prior_image[0],
        (near_image, wide_near_image, wide_far_image), (within,) * 3, (across,) * 3, (within, across),
    )
    far_within, far_across = halos((far_image,))
    fresh, total, w1, g1 = pairs(
        ((1, 0),), stride, table, (far_table,), image, dual, total,
        (far_image,), (far_within,), (far_across,), (within, across), fresh,
    )
    total = settle(total, (near_dual, far_dual), (depth,), (w0, w1), (g0, g1), False)
    volume_next = settle(total, wide, pieces, (w2, w3), (g2, g3), True)
    return (volume_next[None], fresh[None])


def solution(mesh):
    return jax.shard_map(
        shards,
        mesh=mesh,
        in_specs=(
            P("tm", "space", None, None),
            P("tm", "space", None, None),
            P("tm", None, "space", None, None),
            P("tm", None),
            P("tm", None),
        ),
        out_specs=(P("tm", "space", None, None), P("tm", None, "space", None, None)),
        check_vma=False,
    )
```

```python
import functools

import jax
import jax.numpy as jnp
from jax import lax
from jax.experimental import pallas as pl
from jax.experimental.pallas import tpu as pltpu
from jax.sharding import PartitionSpec as P


CYCLES = 8
HOPS = (-2, -1, 1, 2)

dual_step = 0.5
primal_step = 0.25
dual_bound = 0.3
fidelity = 1.0
scale = 1.0 / (1.0 + primal_step * fidelity)
flow = primal_step * scale
patch = -1.0 / (27.0 * 4.0)


LANES = 128
STEP = 32
PARTS = 2
EDGE = 16
RIM = 8


def chosen(table, hop):
    slot = jnp.int32(0)
    filled = table[0] == hop
    for k in range(1, 4):
        hit = table[k] == hop
        slot = jnp.where(hit, k, slot)
        filled = filled | hit
    return slot, filled


def offset_of(table, hop):
    offset = jnp.int32(0)
    for k in range(4):
        offset = jnp.where(table[k] == hop, table[4 + k], offset)
    return offset


def home_slot(table, hop):
    slot, filled = chosen(table, hop)
    count = jnp.int32(0)
    for k in range(4):
        count = count + (table[k] != 0).astype(jnp.int32)
    for other in HOPS:
        _, other_filled = chosen(table, other)
        count = count + ((other < hop) & jnp.logical_not(other_filled)).astype(jnp.int32)
    return jnp.where(filled, slot, count), filled


def hop_of(place, stride):
    width = 1 if place < 2 else 2
    parity = (lax.axis_index("tm") // (stride * width)) % 2
    near = (width * (1 - 2 * parity)).astype(jnp.int32)
    return near if place % 2 == 0 else -near


def piece_of(pieces, z):
    for piece, size in enumerate(pieces):
        if z < size:
            return piece, z
        z -= size


def pack_kernel(places, pieces, stride, table, dual, *refs):
    count = len(places)
    held, sems = refs[-2:]
    refs = list(refs[:-2])
    outs = [[refs.pop(0) for _ in some] for some in pieces]
    depth, rows = dual.shape[1:3]
    moves = []
    for j, place in enumerate(places):
        slot, _ = chosen(table, hop_of(place, stride))
        for half in range(2):
            source = dual.at[slot, :, :, pl.ds(half * LANES, LANES)]
            moves.append(
                pltpu.make_async_copy(source, held.at[j, :, half, pl.ds(RIM, rows), :], sems.at[2 * j + half])
            )
    for m in moves:
        m.start()
    for j in range(count):
        for z in range(depth):
            for half in range(2):
                held[j, z, half, pl.ds(0, RIM), :] = jnp.zeros((RIM, LANES), jnp.float32)
                held[j, z, half, pl.ds(RIM + rows, RIM), :] = jnp.zeros((RIM, LANES), jnp.float32)
    for j, place in enumerate(places):
        offset = offset_of(table, hop_of(place, stride))
        moves[2 * j].wait()
        moves[2 * j + 1].wait()

        def body(step, carry):
            y = pl.multiple_of(step * STEP, STEP)
            for z in range(depth):
                for half in range(2):
                    piece, within = piece_of(pieces[j], z)
                    outs[j][piece][within, pl.ds(y, STEP), pl.ds(half * LANES, LANES)] = held[
                        j, z, half, pl.ds(RIM + y + offset, STEP), :
                    ]
            return carry

        lax.fori_loop(0, rows // STEP, body, 0)


def pack(places, pieces, stride, table, dual):
    _, depth, rows, columns = dual.shape
    count = len(places)
    return pl.pallas_call(
        functools.partial(pack_kernel, places, pieces, stride),
        in_specs=[pl.BlockSpec(memory_space=pltpu.SMEM), pl.BlockSpec(memory_space=pltpu.HBM)],
        out_specs=[pl.BlockSpec(memory_space=pltpu.VMEM)] * sum(map(len, pieces)),
        out_shape=[jax.ShapeDtypeStruct((size, rows, columns), jnp.float32) for some in pieces for size in some],
        scratch_shapes=[
            pltpu.VMEM((count, depth, 2, rows + 2 * RIM, LANES), jnp.float32),
            pltpu.SemaphoreType.DMA((2 * count,)),
        ],
        compiler_params=pltpu.CompilerParams(vmem_limit_bytes=8 << 20),
        cost_estimate=pl.CostEstimate(
            flops=0, bytes_accessed=2 * count * 4 * depth * rows * columns, transcendentals=0
        ),
    )(table, pltpu.with_memory_space_constraint(dual, pltpu.HBM))


def box_rows(sums, z, half, start):
    return (
        sums[z, half, pl.ds(start - 1, STEP), :]
        + sums[z, half, pl.ds(start, STEP), :]
        + sums[z, half, pl.ds(start + 1, STEP), :]
    )


def box_lanes(left, right, lane):
    zero = jnp.zeros_like(left)
    left_up, right_up = pltpu.roll(left, 1, 1), pltpu.roll(right, 1, 1)
    left_down, right_down = pltpu.roll(left, LANES - 1, 1), pltpu.roll(right, LANES - 1, 1)
    first, last = lane == 0, lane == LANES - 1
    return (
        left + jnp.where(first, zero, left_up) + jnp.where(last, right_down, left_down),
        right + jnp.where(first, left_up, right_up) + jnp.where(last, zero, right_down),
    )


def pair_kernel(places, first, stride, table, *refs):
    count = len(places)
    refs = list(refs)
    take = lambda k: [refs.pop(0) for _ in range(k)]
    tables = take(count)
    image, dual, start = take(3)
    partners, inner, outer, own_halos = take(count), take(count), take(count), take(2)
    if not first:
        take(1)
    fresh_out, total = take(2)
    weights, gains = take(count), take(count)
    held, rim, own_sums, in_sums, fresh, sems, out_sems = refs
    depth, rows, _ = image.shape
    f32 = jnp.float32

    even = lax.axis_index("space") % 2 == 0

    def copies(i, upper, lower):
        stacked = places[i][1]
        moves = []
        for half in range(2):
            lanes = pl.ds(half * LANES, LANES)
            moves.append((partners[i].at[:, :, lanes], held.at[i, pl.ds(1, depth), half, pl.ds(EDGE, rows), :]))
            moves.append((upper.at[stacked, :, lanes], held.at[i, 0, half, pl.ds(EDGE, rows), :]))
            moves.append((lower.at[stacked, :, lanes], held.at[i, depth + 1, half, pl.ds(EDGE, rows), :]))
        return [pltpu.make_async_copy(a, b, sems.at[6 * i + j]) for j, (a, b) in enumerate(moves)]

    def start_all(uppers, lowers, own_upper, own_lower):
        for c in rim_copies(own_upper, own_lower):
            c.start()
        for i in range(count):
            for c in copies(i, uppers[i], lowers[i]):
                c.start()

    def rim_copies(upper, lower):
        return [
            pltpu.make_async_copy(upper.at[0], rim.at[0], sems.at[6 * count]),
            pltpu.make_async_copy(lower.at[0], rim.at[1], sems.at[6 * count + 1]),
        ]

    pl.when(even)(lambda: start_all(outer, inner, own_halos[1], own_halos[0]))
    pl.when(jnp.logical_not(even))(lambda: start_all(inner, outer, own_halos[0], own_halos[1]))
    in_copies = [copies(i, inner[i], outer[i]) for i in range(count)]
    for i in range(count):
        for z in range(depth + 2):
            for half in range(2):
                held[i, z, half, pl.ds(0, EDGE), :] = jnp.zeros((EDGE, LANES), f32)
                held[i, z, half, pl.ds(EDGE + rows, EDGE), :] = jnp.zeros((EDGE, LANES), f32)
    for z in range(depth):
        for half in range(2):
            own_sums[z, half, pl.ds(0, RIM), :] = jnp.zeros((RIM, LANES), f32)
            own_sums[z, half, pl.ds(RIM + rows, RIM), :] = jnp.zeros((RIM, LANES), f32)

    row = lax.broadcasted_iota(jnp.int32, (STEP, LANES), 0)
    lane = lax.broadcasted_iota(jnp.int32, (STEP, LANES), 1)

    def mine(z, half, y):
        here, lanes = pl.ds(pl.multiple_of(y, 8), STEP), pl.ds(half * LANES, LANES)
        if z == 0:
            return rim[0, here, lanes]
        if z == depth + 1:
            return rim[1, here, lanes]
        return image[z - 1, here, lanes]

    def store_sums(sums, half, y, size, squares):
        for z in range(depth):
            sums[z, half, pl.ds(pl.multiple_of(RIM + y, 8), size), :] = squares[z] + squares[z + 1] + squares[z + 2]

    for c in rim_copies(*own_halos):
        c.wait()
    out_copies = []
    for i in range(count):
        hop = hop_of(places[i][0], stride)
        source, _ = chosen(table, hop)
        own_offset = offset_of(table, hop)
        slot, filled = home_slot(table, hop)
        bound = jnp.where(filled, f32(dual_bound), f32(0.0))
        _, in_filled = chosen(tables[i], -hop)
        in_offset = offset_of(tables[i], -hop)
        low = jnp.where(in_filled, -in_offset, 4 * rows)
        high = rows - 1 - in_offset
        for c in in_copies[i]:
            c.wait()

        def theirs(z, half, y, shift, size=STEP):
            return held[i, z, half, pl.ds(EDGE + y + shift, size), :]

        for y in (-RIM, rows):
            for half in range(2):
                values = [theirs(z, half, y, in_offset, RIM) for z in range(depth + 2)]
                store_sums(in_sums, half, y, RIM, [v * v for v in values])

        def gather(step, carry):
            y = pl.multiple_of(step * STEP, STEP)
            inside = (row + y >= low) & (row + y <= high)
            for half in range(2):
                own_squares, in_squares = [], []
                for z in range(depth + 2):
                    value = mine(z, half, y)
                    own_square = theirs(z, half, y, -own_offset) - value
                    own_squares.append(own_square * own_square)
                    in_square = jnp.where(inside, value, 0.0) - theirs(z, half, y, in_offset)
                    in_squares.append(in_square * in_square)
                store_sums(own_sums, half, y, STEP, own_squares)
                store_sums(in_sums, half, y, STEP, in_squares)
            return carry

        def apply(step, carry):
            y = pl.multiple_of(step * STEP, STEP)
            inside = (row + y >= low) & (row + y <= high)
            here = pl.ds(y, STEP)
            for z in range(depth):
                own_box = box_lanes(box_rows(own_sums, z, 0, RIM + y), box_rows(own_sums, z, 1, RIM + y), lane)
                in_box = box_lanes(box_rows(in_sums, z, 0, RIM + y), box_rows(in_sums, z, 1, RIM + y), lane)
                for half in range(2):
                    lanes = pl.ds(half * LANES, LANES)
                    value = mine(z + 1, half, y)
                    weight = jnp.exp(own_box[half] * patch)
                    contrast = theirs(z + 1, half, y, -own_offset) - value
                    step_to = dual[source, z, here, lanes] + (dual_step * weight) * contrast
                    step_to = jnp.minimum(jnp.maximum(step_to, -bound), bound)
                    fresh[i, z, here, lanes] = step_to
                    flux = (weight * step_to) * flow
                    if i > 0:
                        total[z, here, lanes] = total[z, here, lanes] + flux
                    elif first:
                        total[z, here, lanes] = scale * value + (flow * fidelity) * start[z, here, lanes] + flux
                    else:
                        total[z, here, lanes] = start[z, here, lanes] + flux
                    weight = jnp.exp(in_box[half] * patch)
                    weights[i][z, here, lanes] = jnp.where(inside, weight, 0.0)
                    gains[i][z, here, lanes] = (dual_step * weight) * (value - theirs(z + 1, half, y, in_offset))
            return carry

        steps = rows // STEP
        lax.fori_loop(0, steps, gather, 0)
        for part in range(PARTS):
            lax.fori_loop(part * steps // PARTS, (part + 1) * steps // PARTS, apply, 0)
            some = pl.ds(part * rows // PARTS, rows // PARTS)
            done = pltpu.make_async_copy(
                fresh.at[i, :, some, :], fresh_out.at[slot, :, some, :], out_sems.at[PARTS * i + part]
            )
            done.start()
            out_copies.append(done)
    for c in out_copies:
        c.wait()


def pairs(places, stride, table, tables, image, dual, start, partners, inner, outer, own_halos, fresh=None):
    count = len(places)
    depth, rows, columns = image.shape
    first = fresh is None
    f32 = jnp.float32
    block = jax.ShapeDtypeStruct(image.shape, f32)
    any_spec = pl.BlockSpec(memory_space=pl.ANY)
    vmem_spec = pl.BlockSpec(memory_space=pltpu.VMEM)
    smem = pl.BlockSpec(memory_space=pltpu.SMEM)
    operands = [table, *tables, image, dual, start, *partners, *inner, *outer, *own_halos]
    specs = [smem] * (1 + count) + [vmem_spec] * 3 + [any_spec] * (3 * count + 2)
    aliases = {}
    if not first:
        aliases = {len(operands): 0}
        operands.append(fresh)
        specs.append(any_spec)
    cells = depth * rows * columns
    return pl.pallas_call(
        functools.partial(pair_kernel, places, first, stride),
        in_specs=specs,
        out_specs=[any_spec] + [vmem_spec] * (1 + 2 * count),
        out_shape=[jax.ShapeDtypeStruct(dual.shape, f32)] + [block] * (1 + 2 * count),
        input_output_aliases=aliases,
        scratch_shapes=[
            pltpu.VMEM((count, depth + 2, 2, rows + 2 * EDGE, LANES), f32),
            pltpu.VMEM((2, rows, columns), f32),
            pltpu.VMEM((depth, 2, rows + 2 * RIM, LANES), f32),
            pltpu.VMEM((depth, 2, rows + 2 * RIM, LANES), f32),
            pltpu.VMEM((count, depth, rows, columns), f32),
            pltpu.SemaphoreType.DMA((6 * count + 2,)),
            pltpu.SemaphoreType.DMA((PARTS * count,)),
        ],
        compiler_params=pltpu.CompilerParams(vmem_limit_bytes=20 << 20),
        cost_estimate=pl.CostEstimate(
            flops=count * 60 * cells, bytes_accessed=4 * (3 + 7 * count) * cells, transcendentals=2 * count * cells
        ),
    )(*operands)


def cut_kernel(*refs):
    count = len(refs) - 3
    images, (within, across, sems) = refs[:count], refs[count:]
    last = images[0].shape[0] - 1
    even = lax.axis_index("space") % 2 == 0

    def copies(inner, outer):
        moves = []
        for k, image in enumerate(images):
            moves.append(pltpu.make_async_copy(image.at[inner], within.at[k], sems.at[2 * k]))
            moves.append(pltpu.make_async_copy(image.at[outer], across.at[k], sems.at[2 * k + 1]))
        return moves

    pl.when(even)(lambda: [c.start() for c in copies(last, 0)] and None)
    pl.when(jnp.logical_not(even))(lambda: [c.start() for c in copies(0, last)] and None)
    for c in copies(last, 0):
        c.wait()


def cut(images):
    count = len(images)
    block = (count,) + images[0].shape[1:]
    return pl.pallas_call(
        cut_kernel,
        in_specs=[pl.BlockSpec(memory_space=pl.ANY)] * count,
        out_specs=[pl.BlockSpec(memory_space=pltpu.VMEM)] * 2,
        out_shape=[jax.ShapeDtypeStruct(block, jnp.float32)] * 2,
        scratch_shapes=[pltpu.SemaphoreType.DMA((2 * count,))],
        compiler_params=pltpu.CompilerParams(vmem_limit_bytes=6 << 20),
        cost_estimate=pl.CostEstimate(flops=0, bytes_accessed=16 * count * block[1] * block[2], transcendentals=0),
    )(*images)


def settle_kernel(terms, slices, kept, total, *refs):
    refs = list(refs)
    take = lambda k: [refs.pop(0) for _ in range(k)]
    duals = [take(len(starts)) for starts in terms]
    weights, gains = take(len(terms)), take(len(terms))
    finished = [z for z in slices if z not in kept]
    if finished:
        out, sems = refs[-2:]
        del refs[-2:]
        result = refs.pop()
    rest = refs[-1] if kept else None
    rows = total.shape[1]
    moves = []
    for z in finished + list(kept):
        here_terms = []
        for k, starts in enumerate(terms):
            for piece, start in enumerate(starts):
                if start <= z < start + duals[k][piece].shape[0]:
                    here_terms.append((duals[k][piece], z - start, weights[k], gains[k]))
        place = kept.index(z) if z in kept else finished.index(z)
        target = rest if z in kept else out

        def body(step, carry):
            here = pl.ds(pl.multiple_of(step * STEP, STEP), STEP)
            arriving = None
            for dual, within, weight, gain in here_terms:
                value = dual[within, here, :] + gain[z, here, :]
                value = weight[z, here, :] * jnp.minimum(jnp.maximum(value, -dual_bound), dual_bound)
                arriving = value if arriving is None else arriving + value
            target[place, here, :] = total[z - slices[0], here, :] - flow * arriving
            return carry

        lax.fori_loop(0, rows // STEP, body, 0)
        if z not in kept:
            moves.append(pltpu.make_async_copy(out.at[place], result.at[z], sems.at[place]))
            moves[-1].start()
    for m in moves:
        m.wait()


def settle(total, terms, slices, kept, depth, result=None):
    vmem_spec, any_spec = pl.BlockSpec(memory_space=pltpu.VMEM), pl.BlockSpec(memory_space=pl.ANY)
    rows, columns = total.shape[1:]
    f32 = jnp.float32
    operands = [total, *(d for t in terms for d in t[0]), *(t[2] for t in terms), *(t[3] for t in terms)]
    specs = [vmem_spec] * len(operands)
    finished = len(slices) - len(kept)
    aliases = {}
    if result is not None:
        aliases = {len(operands): 0}
        operands.append(result)
        specs.append(any_spec)
    shapes, out_specs, scratch = [], [], []
    if kept:
        shapes.append(jax.ShapeDtypeStruct((len(kept), rows, columns), f32))
        out_specs.append(vmem_spec)
    if finished:
        shapes.append(jax.ShapeDtypeStruct((depth, rows, columns), f32))
        out_specs.append(any_spec)
        scratch = [pltpu.VMEM((finished, rows, columns), f32), pltpu.SemaphoreType.DMA((finished,))]
    return pl.pallas_call(
        functools.partial(settle_kernel, tuple(t[1] for t in terms), slices, kept),
        in_specs=specs,
        out_specs=out_specs,
        out_shape=shapes,
        input_output_aliases=aliases,
        scratch_shapes=scratch,
        compiler_params=pltpu.CompilerParams(vmem_limit_bytes=10 << 20),
        cost_estimate=pl.CostEstimate(
            flops=5 * len(terms) * total.size, bytes_accessed=4 * (2 + 3 * len(terms)) * total.size, transcendentals=0
        ),
    )(*operands)


def shards(volume, prior_image, dual_pairs, pair_cycle, pair_offset):
    frames = lax.axis_size("tm")
    spaces = lax.axis_size("space")
    stride = frames // CYCLES
    image = volume[0]
    dual = dual_pairs[0]
    cycle_of = lambda t: t // stride
    every = range(frames)
    swap = [(t, t + stride if cycle_of(t) % 2 == 0 else t - stride) for t in every]
    cross = [(t, t - stride if cycle_of(t) % 2 == 0 else t + stride) for t in every]
    cross = [(a, b) for a, b in cross if 0 <= b < frames]
    wide_swap = [(t, t + 2 * stride if cycle_of(t) // 2 % 2 == 0 else t - 2 * stride) for t in every]
    wide_cross = [(t, t - 2 * stride if cycle_of(t) // 2 % 2 == 0 else t + 2 * stride) for t in every]
    wide_cross = [(a, b) for a, b in wide_cross if 0 <= b < frames]
    relay = [(t, t + 2 * stride if cycle_of(t) % 2 == 0 else t - 2 * stride) for t in every]
    relay = [(a, b) for a, b in relay if 0 <= b < frames]
    inner = [(s, s ^ 1) for s in range(spaces)]
    outer = [(s, s - 1 if s % 2 == 0 else s + 1) for s in range(spaces)]
    outer = [(a, b) for a, b in outer if 0 <= b < spaces]

    def send(x, pairs_, axis="tm"):
        return lax.ppermute(x, axis, pairs_)

    table = jnp.concatenate([pair_cycle[0], pair_offset[0]])

    def halos(images):
        within, across = cut(images)
        return send(within, inner, "space"), send(across, outer, "space")

    near_image = send(image, swap)
    wide_near_image = send(image, wide_swap)
    wide_far_image = send(image, wide_cross)
    near_table = send(table, swap)
    far_table = send(table, cross)
    wide_near_table = send(table, wide_swap)
    wide_far_table = send(table, wide_cross)
    depth = image.shape[0]
    part = max(depth // 4, 1)
    near_dual, far_dual = pack((0, 1), ((depth,),) * 2, stride, table, dual)
    near_dual = send(near_dual, swap)
    far_dual = send(far_dual, cross)
    lead, rest, main, last = pack((2, 3), ((part, depth - part), (depth - part, part)), stride, table, dual)
    lead = send(lead, wide_swap)
    far_image = send(near_image, relay)

    within, across = halos((image, near_image, wide_near_image, wide_far_image))
    main = send(main, wide_cross)
    rest = send(rest, wide_swap)
    last = send(last, wide_cross)
    fresh, total, w0, w2, w3, g0, g2, g3 = pairs(
        ((0, 1), (2, 2), (3, 3)), stride, table, (near_table, wide_near_table, wide_far_table),
        image, dual, prior_image[0],
        (near_image, wide_near_image, wide_far_image), (within,) * 3, (across,) * 3, (within, across),
    )
    far_within, far_across = halos((far_image,))
    fresh, total, w1, g1 = pairs(
        ((1, 0),), stride, table, (far_table,), image, dual, total,
        (far_image,), (far_within,), (far_across,), (within, across), fresh,
    )
    every_slice, late = tuple(range(depth)), tuple(range(depth - part, depth))
    (total,) = settle(
        total, (((near_dual,), (0,), w0, g0), ((far_dual,), (0,), w1, g1)), every_slice, every_slice, depth
    )
    total, volume_next = settle(
        total, (((lead, rest), (0, part), w2, g2), ((main,), (0,), w3, g3)), every_slice, late, depth
    )
    (volume_next,) = settle(total, (((last,), (depth - part,), w3, g3),), late, (), depth, volume_next)
    return (volume_next[None], fresh[None])


def solution(mesh):
    return jax.shard_map(
        shards,
        mesh=mesh,
        in_specs=(
            P("tm", "space", None, None),
            P("tm", "space", None, None),
            P("tm", None, "space", None, None),
            P("tm", None),
            P("tm", None),
        ),
        out_specs=(P("tm", "space", None, None), P("tm", None, "space", None, None)),
        check_vma=False,
    )
```

```python
import functools

import jax
import jax.numpy as jnp
from jax import lax
from jax.experimental import pallas as pl
from jax.experimental.pallas import tpu as pltpu
from jax.sharding import PartitionSpec as P


CYCLES = 8
HOPS = (-2, -1, 1, 2)

dual_step = 0.5
primal_step = 0.25
dual_bound = 0.3
fidelity = 1.0
scale = 1.0 / (1.0 + primal_step * fidelity)
flow = primal_step * scale
patch = -1.0 / (27.0 * 4.0)


LANES = 128
STEP = 32
SHARE = 16
PARTS = 2
EDGE = 16
RIM = 8


def chosen(table, hop):
    slot = jnp.int32(0)
    filled = table[0] == hop
    for k in range(1, 4):
        hit = table[k] == hop
        slot = jnp.where(hit, k, slot)
        filled = filled | hit
    return slot, filled


def offset_of(table, hop):
    offset = jnp.int32(0)
    for k in range(4):
        offset = jnp.where(table[k] == hop, table[4 + k], offset)
    return offset


def home_slot(table, hop):
    slot, filled = chosen(table, hop)
    count = jnp.int32(0)
    for k in range(4):
        count = count + (table[k] != 0).astype(jnp.int32)
    for other in HOPS:
        _, other_filled = chosen(table, other)
        count = count + ((other < hop) & jnp.logical_not(other_filled)).astype(jnp.int32)
    return jnp.where(filled, slot, count), filled


def hop_of(place, stride):
    width = 1 if place < 2 else 2
    parity = (lax.axis_index("tm") // (stride * width)) % 2
    near = (width * (1 - 2 * parity)).astype(jnp.int32)
    return near if place % 2 == 0 else -near


def piece_of(pieces, z):
    for piece, size in enumerate(pieces):
        if z < size:
            return piece, z
        z -= size


def pack_kernel(places, pieces, stride, table, dual, *refs):
    count = len(places)
    held, sems = refs[-2:]
    refs = list(refs[:-2])
    outs = [[refs.pop(0) for _ in some] for some in pieces]
    depth, rows = dual.shape[1:3]
    moves = []
    for j, place in enumerate(places):
        slot, _ = chosen(table, hop_of(place, stride))
        for half in range(2):
            source = dual.at[slot, :, :, pl.ds(half * LANES, LANES)]
            moves.append(
                pltpu.make_async_copy(source, held.at[j, :, half, pl.ds(RIM, rows), :], sems.at[2 * j + half])
            )
    for m in moves:
        m.start()
    for j in range(count):
        for z in range(depth):
            for half in range(2):
                held[j, z, half, pl.ds(0, RIM), :] = jnp.zeros((RIM, LANES), jnp.float32)
                held[j, z, half, pl.ds(RIM + rows, RIM), :] = jnp.zeros((RIM, LANES), jnp.float32)
    for j, place in enumerate(places):
        offset = offset_of(table, hop_of(place, stride))
        moves[2 * j].wait()
        moves[2 * j + 1].wait()

        def body(step, carry):
            y = pl.multiple_of(step * STEP, STEP)
            for z in range(depth):
                for half in range(2):
                    piece, within = piece_of(pieces[j], z)
                    outs[j][piece][within, pl.ds(y, STEP), pl.ds(half * LANES, LANES)] = held[
                        j, z, half, pl.ds(RIM + y + offset, STEP), :
                    ]
            return carry

        lax.fori_loop(0, rows // STEP, body, 0)


def pack(places, pieces, stride, table, dual):
    _, depth, rows, columns = dual.shape
    count = len(places)
    return pl.pallas_call(
        functools.partial(pack_kernel, places, pieces, stride),
        in_specs=[pl.BlockSpec(memory_space=pltpu.SMEM), pl.BlockSpec(memory_space=pltpu.HBM)],
        out_specs=[pl.BlockSpec(memory_space=pltpu.VMEM)] * sum(map(len, pieces)),
        out_shape=[jax.ShapeDtypeStruct((size, rows, columns), jnp.float32) for some in pieces for size in some],
        scratch_shapes=[
            pltpu.VMEM((count, depth, 2, rows + 2 * RIM, LANES), jnp.float32),
            pltpu.SemaphoreType.DMA((2 * count,)),
        ],
        compiler_params=pltpu.CompilerParams(vmem_limit_bytes=8 << 20),
        cost_estimate=pl.CostEstimate(
            flops=0, bytes_accessed=2 * count * 4 * depth * rows * columns, transcendentals=0
        ),
    )(table, pltpu.with_memory_space_constraint(dual, pltpu.HBM))


def box_rows(sums, z, half, start):
    return (
        sums[z, half, pl.ds(start - 1, STEP), :]
        + sums[z, half, pl.ds(start, STEP), :]
        + sums[z, half, pl.ds(start + 1, STEP), :]
    )


def box_lanes(left, right, lane):
    zero = jnp.zeros_like(left)
    left_up, right_up = pltpu.roll(left, 1, 1), pltpu.roll(right, 1, 1)
    left_down, right_down = pltpu.roll(left, LANES - 1, 1), pltpu.roll(right, LANES - 1, 1)
    first, last = lane == 0, lane == LANES - 1
    return (
        left + jnp.where(first, zero, left_up) + jnp.where(last, right_down, left_down),
        right + jnp.where(first, left_up, right_up) + jnp.where(last, zero, right_down),
    )


def pair_kernel(places, parts, first, stride, table, *refs):
    count = len(places)
    refs = list(refs)
    take = lambda k: [refs.pop(0) for _ in range(k)]
    tables = take(count)
    image, dual, start = take(3)
    partners = [take(k) for k in parts]
    inner, outer, own_halos = take(count), take(count), take(2)
    if not first:
        take(1)
    fresh_out, total = take(2)
    weights, gains = take(count), take(count)
    held, rim, own_sums, in_sums, fresh, sems, out_sems = refs
    depth, rows, _ = image.shape
    f32 = jnp.float32

    even = lax.axis_index("space") % 2 == 0

    def copies(i, upper, lower):
        stacked = places[i][1]
        moves = []
        for half in range(2):
            lanes = pl.ds(half * LANES, LANES)
            top = EDGE
            for part in partners[i]:
                moves.append((part.at[:, :, lanes], held.at[i, pl.ds(1, depth), half, pl.ds(top, part.shape[1]), :]))
                top += part.shape[1]
            moves.append((upper.at[stacked, :, lanes], held.at[i, 0, half, pl.ds(EDGE, rows), :]))
            moves.append((lower.at[stacked, :, lanes], held.at[i, depth + 1, half, pl.ds(EDGE, rows), :]))
        return [pltpu.make_async_copy(a, b, sems.at[8 * i + j]) for j, (a, b) in enumerate(moves)]

    def start_all(uppers, lowers, own_upper, own_lower):
        for c in rim_copies(own_upper, own_lower):
            c.start()
        for i in range(count):
            for c in copies(i, uppers[i], lowers[i]):
                c.start()

    def rim_copies(upper, lower):
        return [
            pltpu.make_async_copy(upper.at[0], rim.at[0], sems.at[8 * count]),
            pltpu.make_async_copy(lower.at[0], rim.at[1], sems.at[8 * count + 1]),
        ]

    pl.when(even)(lambda: start_all(outer, inner, own_halos[1], own_halos[0]))
    pl.when(jnp.logical_not(even))(lambda: start_all(inner, outer, own_halos[0], own_halos[1]))
    in_copies = [copies(i, inner[i], outer[i]) for i in range(count)]
    for i in range(count):
        for z in range(depth + 2):
            for half in range(2):
                held[i, z, half, pl.ds(0, EDGE), :] = jnp.zeros((EDGE, LANES), f32)
                held[i, z, half, pl.ds(EDGE + rows, EDGE), :] = jnp.zeros((EDGE, LANES), f32)
    for z in range(depth):
        for half in range(2):
            own_sums[z, half, pl.ds(0, RIM), :] = jnp.zeros((RIM, LANES), f32)
            own_sums[z, half, pl.ds(RIM + rows, RIM), :] = jnp.zeros((RIM, LANES), f32)

    row = lax.broadcasted_iota(jnp.int32, (STEP, LANES), 0)
    lane = lax.broadcasted_iota(jnp.int32, (STEP, LANES), 1)

    def mine(z, half, y):
        here, lanes = pl.ds(pl.multiple_of(y, 8), STEP), pl.ds(half * LANES, LANES)
        if z == 0:
            return rim[0, here, lanes]
        if z == depth + 1:
            return rim[1, here, lanes]
        return image[z - 1, here, lanes]

    def store_sums(sums, half, y, size, squares):
        for z in range(depth):
            sums[z, half, pl.ds(pl.multiple_of(RIM + y, 8), size), :] = squares[z] + squares[z + 1] + squares[z + 2]

    for c in rim_copies(*own_halos):
        c.wait()
    out_copies = []
    for i in range(count):
        hop = hop_of(places[i][0], stride)
        source, _ = chosen(table, hop)
        own_offset = offset_of(table, hop)
        slot, filled = home_slot(table, hop)
        bound = jnp.where(filled, f32(dual_bound), f32(0.0))
        _, in_filled = chosen(tables[i], -hop)
        in_offset = offset_of(tables[i], -hop)
        low = jnp.where(in_filled, -in_offset, 4 * rows)
        high = rows - 1 - in_offset
        for c in in_copies[i]:
            c.wait()

        def theirs(z, half, y, shift, size=STEP):
            return held[i, z, half, pl.ds(EDGE + y + shift, size), :]

        for y in (-RIM, rows):
            for half in range(2):
                values = [theirs(z, half, y, in_offset, RIM) for z in range(depth + 2)]
                store_sums(in_sums, half, y, RIM, [v * v for v in values])

        def gather(step, carry):
            y = pl.multiple_of(step * STEP, STEP)
            inside = (row + y >= low) & (row + y <= high)
            for half in range(2):
                own_squares, in_squares = [], []
                for z in range(depth + 2):
                    value = mine(z, half, y)
                    own_square = theirs(z, half, y, -own_offset) - value
                    own_squares.append(own_square * own_square)
                    in_square = jnp.where(inside, value, 0.0) - theirs(z, half, y, in_offset)
                    in_squares.append(in_square * in_square)
                store_sums(own_sums, half, y, STEP, own_squares)
                store_sums(in_sums, half, y, STEP, in_squares)
            return carry

        def apply(step, carry):
            y = pl.multiple_of(step * STEP, STEP)
            inside = (row + y >= low) & (row + y <= high)
            here = pl.ds(y, STEP)
            for z in range(depth):
                own_box = box_lanes(box_rows(own_sums, z, 0, RIM + y), box_rows(own_sums, z, 1, RIM + y), lane)
                in_box = box_lanes(box_rows(in_sums, z, 0, RIM + y), box_rows(in_sums, z, 1, RIM + y), lane)
                for half in range(2):
                    lanes = pl.ds(half * LANES, LANES)
                    value = mine(z + 1, half, y)
                    weight = jnp.exp(own_box[half] * patch)
                    contrast = theirs(z + 1, half, y, -own_offset) - value
                    step_to = dual[source, z, here, lanes] + (dual_step * weight) * contrast
                    step_to = jnp.minimum(jnp.maximum(step_to, -bound), bound)
                    fresh[i, z, here, lanes] = step_to
                    flux = (weight * step_to) * flow
                    if i > 0:
                        total[z, here, lanes] = total[z, here, lanes] + flux
                    elif first:
                        total[z, here, lanes] = scale * value + (flow * fidelity) * start[z, here, lanes] + flux
                    else:
                        total[z, here, lanes] = start[z, here, lanes] + flux
                    weight = jnp.exp(in_box[half] * patch)
                    weights[i][z, here, lanes] = jnp.where(inside, weight, 0.0)
                    gains[i][z, here, lanes] = (dual_step * weight) * (value - theirs(z + 1, half, y, in_offset))
            return carry

        steps = rows // STEP
        lax.fori_loop(0, steps, gather, 0)
        for part in range(PARTS):
            lax.fori_loop(part * steps // PARTS, (part + 1) * steps // PARTS, apply, 0)
            some = pl.ds(part * rows // PARTS, rows // PARTS)
            done = pltpu.make_async_copy(
                fresh.at[i, :, some, :], fresh_out.at[slot, :, some, :], out_sems.at[PARTS * i + part]
            )
            done.start()
            out_copies.append(done)
    for c in out_copies:
        c.wait()


def pairs(places, stride, table, tables, image, dual, start, partners, inner, outer, own_halos, fresh=None):
    count = len(places)
    depth, rows, columns = image.shape
    first = fresh is None
    f32 = jnp.float32
    block = jax.ShapeDtypeStruct(image.shape, f32)
    any_spec = pl.BlockSpec(memory_space=pl.ANY)
    vmem_spec = pl.BlockSpec(memory_space=pltpu.VMEM)
    smem = pl.BlockSpec(memory_space=pltpu.SMEM)
    parts = tuple(map(len, partners))
    partners = [part for partner in partners for part in partner]
    operands = [table, *tables, image, dual, start, *partners, *inner, *outer, *own_halos]
    specs = [smem] * (1 + count) + [vmem_spec] * 3 + [any_spec] * (len(partners) + 2 * count + 2)
    aliases = {}
    if not first:
        aliases = {len(operands): 0}
        operands.append(fresh)
        specs.append(any_spec)
    cells = depth * rows * columns
    return pl.pallas_call(
        functools.partial(pair_kernel, places, parts, first, stride),
        in_specs=specs,
        out_specs=[any_spec] + [vmem_spec] * (1 + 2 * count),
        out_shape=[jax.ShapeDtypeStruct(dual.shape, f32)] + [block] * (1 + 2 * count),
        input_output_aliases=aliases,
        scratch_shapes=[
            pltpu.VMEM((count, depth + 2, 2, rows + 2 * EDGE, LANES), f32),
            pltpu.VMEM((2, rows, columns), f32),
            pltpu.VMEM((depth, 2, rows + 2 * RIM, LANES), f32),
            pltpu.VMEM((depth, 2, rows + 2 * RIM, LANES), f32),
            pltpu.VMEM((count, depth, rows, columns), f32),
            pltpu.SemaphoreType.DMA((8 * count + 2,)),
            pltpu.SemaphoreType.DMA((PARTS * count,)),
        ],
        compiler_params=pltpu.CompilerParams(vmem_limit_bytes=20 << 20),
        cost_estimate=pl.CostEstimate(
            flops=count * 60 * cells, bytes_accessed=4 * (3 + 7 * count) * cells, transcendentals=2 * count * cells
        ),
    )(*operands)


def cut_kernel(parts, *refs):
    refs = list(refs)
    images = [[refs.pop(0) for _ in range(k)] for k in parts]
    within, across, sems = refs
    last = images[0][0].shape[0] - 1
    even = lax.axis_index("space") % 2 == 0

    def copies(inner, outer):
        moves = []
        for k, image in enumerate(images):
            top = 0
            for part in image:
                some = pl.ds(top, part.shape[1])
                for source, target in ((part.at[inner], within), (part.at[outer], across)):
                    moves.append(pltpu.make_async_copy(source, target.at[k, some, :], sems.at[len(moves)]))
                top += part.shape[1]
        return moves

    pl.when(even)(lambda: [c.start() for c in copies(last, 0)] and None)
    pl.when(jnp.logical_not(even))(lambda: [c.start() for c in copies(0, last)] and None)
    for c in copies(last, 0):
        c.wait()


def cut(images):
    parts = tuple(map(len, images))
    rows = sum(part.shape[1] for part in images[0])
    block = (len(images), rows, images[0][0].shape[2])
    return pl.pallas_call(
        functools.partial(cut_kernel, parts),
        in_specs=[pl.BlockSpec(memory_space=pl.ANY)] * sum(parts),
        out_specs=[pl.BlockSpec(memory_space=pltpu.VMEM)] * 2,
        out_shape=[jax.ShapeDtypeStruct(block, jnp.float32)] * 2,
        scratch_shapes=[pltpu.SemaphoreType.DMA((2 * sum(parts),))],
        compiler_params=pltpu.CompilerParams(vmem_limit_bytes=6 << 20),
        cost_estimate=pl.CostEstimate(flops=0, bytes_accessed=16 * len(images) * block[1] * block[2], transcendentals=0),
    )(*(part for image in images for part in image))


def rows_kernel(top, image, out, sem):
    copy = pltpu.make_async_copy(image.at[:, pl.ds(top, out.shape[1]), :], out, sem)
    copy.start()
    copy.wait()


def shift_kernel(stride, wide_near, wide_far, out, sem):
    cycle = lax.axis_index("tm") // stride
    same = cycle % 2 == cycle // 2 % 2
    some = pl.ds(0, out.shape[1])
    near_copy = pltpu.make_async_copy(wide_near.at[:, some, :], out, sem)
    far_copy = pltpu.make_async_copy(wide_far.at[:, some, :], out, sem)
    pl.when(same)(near_copy.start)
    pl.when(jnp.logical_not(same))(far_copy.start)
    near_copy.wait()


def rows_of(kernel, images, size):
    depth, _, columns = images[0].shape
    return pl.pallas_call(
        kernel,
        in_specs=[pl.BlockSpec(memory_space=pl.ANY)] * len(images),
        out_specs=pl.BlockSpec(memory_space=pltpu.VMEM),
        out_shape=jax.ShapeDtypeStruct((depth, size, columns), jnp.float32),
        scratch_shapes=[pltpu.SemaphoreType.DMA],
        compiler_params=pltpu.CompilerParams(vmem_limit_bytes=4 << 20),
        cost_estimate=pl.CostEstimate(flops=0, bytes_accessed=8 * depth * size * columns, transcendentals=0),
    )(*images)


def settle_kernel(terms, slices, kept, total, *refs):
    refs = list(refs)
    take = lambda k: [refs.pop(0) for _ in range(k)]
    duals = [take(len(starts)) for starts in terms]
    weights, gains = take(len(terms)), take(len(terms))
    finished = [z for z in slices if z not in kept]
    if finished:
        out, sems = refs[-2:]
        del refs[-2:]
        result = refs.pop()
    rest = refs[-1] if kept else None
    rows = total.shape[1]
    moves = []
    for z in finished + list(kept):
        here_terms = []
        for k, starts in enumerate(terms):
            for piece, start in enumerate(starts):
                if start <= z < start + duals[k][piece].shape[0]:
                    here_terms.append((duals[k][piece], z - start, weights[k], gains[k]))
        place = kept.index(z) if z in kept else finished.index(z)
        target = rest if z in kept else out

        def body(step, carry):
            here = pl.ds(pl.multiple_of(step * STEP, STEP), STEP)
            arriving = None
            for dual, within, weight, gain in here_terms:
                value = dual[within, here, :] + gain[z, here, :]
                value = weight[z, here, :] * jnp.minimum(jnp.maximum(value, -dual_bound), dual_bound)
                arriving = value if arriving is None else arriving + value
            target[place, here, :] = total[z - slices[0], here, :] - flow * arriving
            return carry

        lax.fori_loop(0, rows // STEP, body, 0)
        if z not in kept:
            moves.append(pltpu.make_async_copy(out.at[place], result.at[z], sems.at[place]))
            moves[-1].start()
    for m in moves:
        m.wait()


def settle(total, terms, slices, kept, depth, result=None):
    vmem_spec, any_spec = pl.BlockSpec(memory_space=pltpu.VMEM), pl.BlockSpec(memory_space=pl.ANY)
    rows, columns = total.shape[1:]
    f32 = jnp.float32
    operands = [total, *(d for t in terms for d in t[0]), *(t[2] for t in terms), *(t[3] for t in terms)]
    specs = [vmem_spec] * len(operands)
    finished = len(slices) - len(kept)
    aliases = {}
    if result is not None:
        aliases = {len(operands): 0}
        operands.append(result)
        specs.append(any_spec)
    shapes, out_specs, scratch = [], [], []
    if kept:
        shapes.append(jax.ShapeDtypeStruct((len(kept), rows, columns), f32))
        out_specs.append(vmem_spec)
    if finished:
        shapes.append(jax.ShapeDtypeStruct((depth, rows, columns), f32))
        out_specs.append(any_spec)
        scratch = [pltpu.VMEM((finished, rows, columns), f32), pltpu.SemaphoreType.DMA((finished,))]
    return pl.pallas_call(
        functools.partial(settle_kernel, tuple(t[1] for t in terms), slices, kept),
        in_specs=specs,
        out_specs=out_specs,
        out_shape=shapes,
        input_output_aliases=aliases,
        scratch_shapes=scratch,
        compiler_params=pltpu.CompilerParams(vmem_limit_bytes=10 << 20),
        cost_estimate=pl.CostEstimate(
            flops=5 * len(terms) * total.size, bytes_accessed=4 * (2 + 3 * len(terms)) * total.size, transcendentals=0
        ),
    )(*operands)


def shards(volume, prior_image, dual_pairs, pair_cycle, pair_offset):
    frames = lax.axis_size("tm")
    spaces = lax.axis_size("space")
    stride = frames // CYCLES
    image = volume[0]
    dual = dual_pairs[0]
    cycle_of = lambda t: t // stride
    every = range(frames)
    swap = [(t, t + stride if cycle_of(t) % 2 == 0 else t - stride) for t in every]
    cross = [(t, t - stride if cycle_of(t) % 2 == 0 else t + stride) for t in every]
    cross = [(a, b) for a, b in cross if 0 <= b < frames]
    wide_swap = [(t, t + 2 * stride if cycle_of(t) // 2 % 2 == 0 else t - 2 * stride) for t in every]
    wide_cross = [(t, t - 2 * stride if cycle_of(t) // 2 % 2 == 0 else t + 2 * stride) for t in every]
    wide_cross = [(a, b) for a, b in wide_cross if 0 <= b < frames]
    relay = [(t, t + 2 * stride if cycle_of(t) % 2 == 0 else t - 2 * stride) for t in every]
    relay = [(a, b) for a, b in relay if 0 <= b < frames]
    inner = [(s, s ^ 1) for s in range(spaces)]
    outer = [(s, s - 1 if s % 2 == 0 else s + 1) for s in range(spaces)]
    outer = [(a, b) for a, b in outer if 0 <= b < spaces]

    def send(x, pairs_, axis="tm"):
        return lax.ppermute(x, axis, pairs_)

    table = jnp.concatenate([pair_cycle[0], pair_offset[0]])

    def halos(images):
        within, across = cut(images)
        return send(within, inner, "space"), send(across, outer, "space")

    near_image = send(image, swap)
    wide_near_image = send(image, wide_swap)
    wide_far_image = send(image, wide_cross)
    near_table = send(table, swap)
    far_table = send(table, cross)
    wide_near_table = send(table, wide_swap)
    wide_far_table = send(table, wide_cross)
    depth = image.shape[0]
    part = max(depth // 4, 1)
    near_lead, near_rest, far_dual = pack((0, 1), ((part, depth - part), (depth,)), stride, table, dual)
    near_lead = send(near_lead, swap)
    far_dual = send(far_dual, cross)
    lead, rest, main, last = pack((2, 3), ((part, depth - part), (depth - part, part)), stride, table, dual)
    lead = send(lead, wide_swap)
    rows = image.shape[1]
    ahead = rows // SHARE // 8 * 8
    relayed = rows_of(functools.partial(rows_kernel, ahead), (near_image,), rows - ahead)
    relayed = send(relayed, relay)
    within, across = halos(((image,), (near_image,), (wide_near_image,), (wide_far_image,)))
    shifted = rows_of(functools.partial(shift_kernel, stride), (wide_near_image, wide_far_image), ahead)
    shifted = send(shifted, swap)
    far_image = (shifted, relayed)
    main = send(main, wide_cross)
    near_rest = send(near_rest, swap)
    rest = send(rest, wide_swap)
    last = send(last, wide_cross)
    fresh, total, w0, w2, w3, g0, g2, g3 = pairs(
        ((0, 1), (2, 2), (3, 3)), stride, table, (near_table, wide_near_table, wide_far_table),
        image, dual, prior_image[0],
        ((near_image,), (wide_near_image,), (wide_far_image,)), (within,) * 3, (across,) * 3, (within, across),
    )
    far_within, far_across = halos((far_image,))
    fresh, total, w1, g1 = pairs(
        ((1, 0),), stride, table, (far_table,), image, dual, total,
        (far_image,), (far_within,), (far_across,), (within, across), fresh,
    )
    every_slice, late = tuple(range(depth)), tuple(range(depth - part, depth))
    (total,) = settle(
        total, (((near_lead, near_rest), (0, part), w0, g0), ((far_dual,), (0,), w1, g1)), every_slice, every_slice, depth
    )
    total, volume_next = settle(
        total, (((lead, rest), (0, part), w2, g2), ((main,), (0,), w3, g3)), every_slice, late, depth
    )
    (volume_next,) = settle(total, (((last,), (depth - part,), w3, g3),), late, (), depth, volume_next)
    return (volume_next[None], fresh[None])


def solution(mesh):
    return jax.shard_map(
        shards,
        mesh=mesh,
        in_specs=(
            P("tm", "space", None, None),
            P("tm", "space", None, None),
            P("tm", None, "space", None, None),
            P("tm", None),
            P("tm", None),
        ),
        out_specs=(P("tm", "space", None, None), P("tm", None, "space", None, None)),
        check_vma=False,
    )
```

```python
import functools

import jax
import jax.numpy as jnp
from jax import lax
from jax.experimental import pallas as pl
from jax.experimental.pallas import tpu as pltpu
from jax.sharding import PartitionSpec as P


CYCLES = 8
HOPS = (-2, -1, 1, 2)

dual_step = 0.5
primal_step = 0.25
dual_bound = 0.3
fidelity = 1.0
scale = 1.0 / (1.0 + primal_step * fidelity)
flow = primal_step * scale
patch = -1.0 / (27.0 * 4.0)


LANES = 128
STEP = 32
SETTLE = 256
PARTS = 2
EDGE = 16
RIM = 8


def chosen(table, hop):
    slot = jnp.int32(0)
    filled = table[0] == hop
    for k in range(1, 4):
        hit = table[k] == hop
        slot = jnp.where(hit, k, slot)
        filled = filled | hit
    return slot, filled


def offset_of(table, hop):
    offset = jnp.int32(0)
    for k in range(4):
        offset = jnp.where(table[k] == hop, table[4 + k], offset)
    return offset


def home_slot(table, hop):
    slot, filled = chosen(table, hop)
    count = jnp.int32(0)
    for k in range(4):
        count = count + (table[k] != 0).astype(jnp.int32)
    for other in HOPS:
        _, other_filled = chosen(table, other)
        count = count + ((other < hop) & jnp.logical_not(other_filled)).astype(jnp.int32)
    return jnp.where(filled, slot, count), filled


def hop_of(place, stride):
    width = 1 if place < 2 else 2
    parity = (lax.axis_index("tm") // (stride * width)) % 2
    near = (width * (1 - 2 * parity)).astype(jnp.int32)
    return near if place % 2 == 0 else -near


def piece_of(pieces, z):
    for piece, size in enumerate(pieces):
        if z < size:
            return piece, z
        z -= size


def pack_kernel(places, pieces, stride, table, dual, *refs):
    count = len(places)
    held, sems = refs[-2:]
    refs = list(refs[:-2])
    outs = [[refs.pop(0) for _ in some] for some in pieces]
    depth, rows = dual.shape[1:3]
    moves = []
    for j, place in enumerate(places):
        slot, _ = chosen(table, hop_of(place, stride))
        for half in range(2):
            source = dual.at[slot, :, :, pl.ds(half * LANES, LANES)]
            moves.append(
                pltpu.make_async_copy(source, held.at[j, :, half, pl.ds(RIM, rows), :], sems.at[2 * j + half])
            )
    for m in moves:
        m.start()
    for j in range(count):
        for z in range(depth):
            for half in range(2):
                held[j, z, half, pl.ds(0, RIM), :] = jnp.zeros((RIM, LANES), jnp.float32)
                held[j, z, half, pl.ds(RIM + rows, RIM), :] = jnp.zeros((RIM, LANES), jnp.float32)
    for j, place in enumerate(places):
        offset = offset_of(table, hop_of(place, stride))
        moves[2 * j].wait()
        moves[2 * j + 1].wait()

        def body(step, carry):
            y = pl.multiple_of(step * STEP, STEP)
            for z in range(depth):
                for half in range(2):
                    piece, within = piece_of(pieces[j], z)
                    outs[j][piece][within, pl.ds(y, STEP), pl.ds(half * LANES, LANES)] = held[
                        j, z, half, pl.ds(RIM + y + offset, STEP), :
                    ]
            return carry

        lax.fori_loop(0, rows // STEP, body, 0)


def pack(places, pieces, stride, table, dual):
    _, depth, rows, columns = dual.shape
    count = len(places)
    return pl.pallas_call(
        functools.partial(pack_kernel, places, pieces, stride),
        in_specs=[pl.BlockSpec(memory_space=pltpu.SMEM), pl.BlockSpec(memory_space=pltpu.HBM)],
        out_specs=[pl.BlockSpec(memory_space=pltpu.VMEM)] * sum(map(len, pieces)),
        out_shape=[jax.ShapeDtypeStruct((size, rows, columns), jnp.float32) for some in pieces for size in some],
        scratch_shapes=[
            pltpu.VMEM((count, depth, 2, rows + 2 * RIM, LANES), jnp.float32),
            pltpu.SemaphoreType.DMA((2 * count,)),
        ],
        compiler_params=pltpu.CompilerParams(vmem_limit_bytes=8 << 20),
        cost_estimate=pl.CostEstimate(
            flops=0, bytes_accessed=2 * count * 4 * depth * rows * columns, transcendentals=0
        ),
    )(table, pltpu.with_memory_space_constraint(dual, pltpu.HBM))


def box_rows(sums, z, half, start):
    return (
        sums[z, half, pl.ds(start - 1, STEP), :]
        + sums[z, half, pl.ds(start, STEP), :]
        + sums[z, half, pl.ds(start + 1, STEP), :]
    )


def box_lanes(left, right, lane):
    zero = jnp.zeros_like(left)
    left_up, right_up = pltpu.roll(left, 1, 1), pltpu.roll(right, 1, 1)
    left_down, right_down = pltpu.roll(left, LANES - 1, 1), pltpu.roll(right, LANES - 1, 1)
    first, last = lane == 0, lane == LANES - 1
    return (
        left + jnp.where(first, zero, left_up) + jnp.where(last, right_down, left_down),
        right + jnp.where(first, left_up, right_up) + jnp.where(last, zero, right_down),
    )


def pair_kernel(places, first, stride, table, *refs):
    count = len(places)
    refs = list(refs)
    take = lambda k: [refs.pop(0) for _ in range(k)]
    tables = take(count)
    image, dual, start = take(3)
    partners, inner, outer, own_halos = take(count), take(count), take(count), take(2)
    if not first:
        take(1)
    fresh_out, total = take(2)
    weights, gains = take(count), take(count)
    held, rim, own_sums, in_sums, fresh, sems, out_sems = refs
    depth, rows, _ = image.shape
    f32 = jnp.float32

    even = lax.axis_index("space") % 2 == 0

    def copies(i, upper, lower):
        stacked = places[i][1]
        moves = []
        for half in range(2):
            lanes = pl.ds(half * LANES, LANES)
            moves.append((partners[i].at[:, :, lanes], held.at[i, pl.ds(1, depth), half, pl.ds(EDGE, rows), :]))
            moves.append((upper.at[stacked, :, lanes], held.at[i, 0, half, pl.ds(EDGE, rows), :]))
            moves.append((lower.at[stacked, :, lanes], held.at[i, depth + 1, half, pl.ds(EDGE, rows), :]))
        return [pltpu.make_async_copy(a, b, sems.at[6 * i + j]) for j, (a, b) in enumerate(moves)]

    def start_all(uppers, lowers, own_upper, own_lower):
        for c in rim_copies(own_upper, own_lower):
            c.start()
        for i in range(count):
            for c in copies(i, uppers[i], lowers[i]):
                c.start()

    def rim_copies(upper, lower):
        return [
            pltpu.make_async_copy(upper.at[0], rim.at[0], sems.at[6 * count]),
            pltpu.make_async_copy(lower.at[0], rim.at[1], sems.at[6 * count + 1]),
        ]

    pl.when(even)(lambda: start_all(outer, inner, own_halos[1], own_halos[0]))
    pl.when(jnp.logical_not(even))(lambda: start_all(inner, outer, own_halos[0], own_halos[1]))
    in_copies = [copies(i, inner[i], outer[i]) for i in range(count)]
    for i in range(count):
        for z in range(depth + 2):
            for half in range(2):
                held[i, z, half, pl.ds(0, EDGE), :] = jnp.zeros((EDGE, LANES), f32)
                held[i, z, half, pl.ds(EDGE + rows, EDGE), :] = jnp.zeros((EDGE, LANES), f32)
    for z in range(depth):
        for half in range(2):
            own_sums[z, half, pl.ds(0, RIM), :] = jnp.zeros((RIM, LANES), f32)
            own_sums[z, half, pl.ds(RIM + rows, RIM), :] = jnp.zeros((RIM, LANES), f32)

    row = lax.broadcasted_iota(jnp.int32, (STEP, LANES), 0)
    lane = lax.broadcasted_iota(jnp.int32, (STEP, LANES), 1)

    def mine(z, half, y):
        here, lanes = pl.ds(pl.multiple_of(y, 8), STEP), pl.ds(half * LANES, LANES)
        if z == 0:
            return rim[0, here, lanes]
        if z == depth + 1:
            return rim[1, here, lanes]
        return image[z - 1, here, lanes]

    def store_sums(sums, half, y, size, squares):
        for z in range(depth):
            sums[z, half, pl.ds(pl.multiple_of(RIM + y, 8), size), :] = squares[z] + squares[z + 1] + squares[z + 2]

    for c in rim_copies(*own_halos):
        c.wait()
    out_copies = []
    for i in range(count):
        hop = hop_of(places[i][0], stride)
        source, _ = chosen(table, hop)
        own_offset = offset_of(table, hop)
        slot, filled = home_slot(table, hop)
        bound = jnp.where(filled, f32(dual_bound), f32(0.0))
        _, in_filled = chosen(tables[i], -hop)
        partner = lax.axis_index("tm") // stride + hop
        in_filled = in_filled & (partner >= 0) & (partner < CYCLES)
        in_offset = offset_of(tables[i], -hop)
        low = jnp.where(in_filled, -in_offset, 4 * rows)
        high = rows - 1 - in_offset
        for c in in_copies[i]:
            c.wait()

        def theirs(z, half, y, shift, size=STEP):
            return held[i, z, half, pl.ds(EDGE + y + shift, size), :]

        for y in (-RIM, rows):
            for half in range(2):
                values = [theirs(z, half, y, in_offset, RIM) for z in range(depth + 2)]
                store_sums(in_sums, half, y, RIM, [v * v for v in values])

        def gather(step, carry):
            y = pl.multiple_of(step * STEP, STEP)
            inside = (row + y >= low) & (row + y <= high)
            for half in range(2):
                own_squares, in_squares = [], []
                for z in range(depth + 2):
                    value = mine(z, half, y)
                    own_square = theirs(z, half, y, -own_offset) - value
                    own_squares.append(own_square * own_square)
                    in_square = jnp.where(inside, value, 0.0) - theirs(z, half, y, in_offset)
                    in_squares.append(in_square * in_square)
                store_sums(own_sums, half, y, STEP, own_squares)
                store_sums(in_sums, half, y, STEP, in_squares)
            return carry

        def apply(step, carry):
            y = pl.multiple_of(step * STEP, STEP)
            inside = (row + y >= low) & (row + y <= high)
            here = pl.ds(y, STEP)
            for z in range(depth):
                own_box = box_lanes(box_rows(own_sums, z, 0, RIM + y), box_rows(own_sums, z, 1, RIM + y), lane)
                in_box = box_lanes(box_rows(in_sums, z, 0, RIM + y), box_rows(in_sums, z, 1, RIM + y), lane)
                for half in range(2):
                    lanes = pl.ds(half * LANES, LANES)
                    value = mine(z + 1, half, y)
                    weight = jnp.exp(own_box[half] * patch)
                    contrast = theirs(z + 1, half, y, -own_offset) - value
                    step_to = dual[source, z, here, lanes] + (dual_step * weight) * contrast
                    step_to = jnp.minimum(jnp.maximum(step_to, -bound), bound)
                    fresh[i, z, here, lanes] = step_to
                    flux = (weight * step_to) * flow
                    if i > 0:
                        total[z, here, lanes] = total[z, here, lanes] + flux
                    elif first:
                        total[z, here, lanes] = scale * value + (flow * fidelity) * start[z, here, lanes] + flux
                    else:
                        total[z, here, lanes] = start[z, here, lanes] + flux
                    weight = jnp.exp(in_box[half] * patch)
                    weights[i][z, here, lanes] = jnp.where(inside, weight, 0.0)
                    gains[i][z, here, lanes] = (dual_step * weight) * (value - theirs(z + 1, half, y, in_offset))
            return carry

        steps = rows // STEP
        lax.fori_loop(0, steps, gather, 0)
        for part in range(PARTS):
            lax.fori_loop(part * steps // PARTS, (part + 1) * steps // PARTS, apply, 0)
            some = pl.ds(part * rows // PARTS, rows // PARTS)
            done = pltpu.make_async_copy(
                fresh.at[i, :, some, :], fresh_out.at[slot, :, some, :], out_sems.at[PARTS * i + part]
            )
            done.start()
            out_copies.append(done)
    for c in out_copies:
        c.wait()


def pairs(places, stride, table, tables, image, dual, start, partners, inner, outer, own_halos, fresh=None):
    count = len(places)
    depth, rows, columns = image.shape
    first = fresh is None
    f32 = jnp.float32
    block = jax.ShapeDtypeStruct(image.shape, f32)
    any_spec = pl.BlockSpec(memory_space=pl.ANY)
    vmem_spec = pl.BlockSpec(memory_space=pltpu.VMEM)
    smem = pl.BlockSpec(memory_space=pltpu.SMEM)
    operands = [table, *tables, image, dual, start, *partners, *inner, *outer, *own_halos]
    specs = [smem] * (1 + count) + [vmem_spec] * 3 + [any_spec] * (3 * count + 2)
    aliases = {}
    if not first:
        aliases = {len(operands): 0}
        operands.append(fresh)
        specs.append(any_spec)
    cells = depth * rows * columns
    return pl.pallas_call(
        functools.partial(pair_kernel, places, first, stride),
        in_specs=specs,
        out_specs=[any_spec] + [vmem_spec] * (1 + 2 * count),
        out_shape=[jax.ShapeDtypeStruct(dual.shape, f32)] + [block] * (1 + 2 * count),
        input_output_aliases=aliases,
        scratch_shapes=[
            pltpu.VMEM((count, depth + 2, 2, rows + 2 * EDGE, LANES), f32),
            pltpu.VMEM((2, rows, columns), f32),
            pltpu.VMEM((depth, 2, rows + 2 * RIM, LANES), f32),
            pltpu.VMEM((depth, 2, rows + 2 * RIM, LANES), f32),
            pltpu.VMEM((count, depth, rows, columns), f32),
            pltpu.SemaphoreType.DMA((6 * count + 2,)),
            pltpu.SemaphoreType.DMA((PARTS * count,)),
        ],
        compiler_params=pltpu.CompilerParams(vmem_limit_bytes=20 << 20),
        cost_estimate=pl.CostEstimate(
            flops=count * 60 * cells, bytes_accessed=4 * (3 + 7 * count) * cells, transcendentals=2 * count * cells
        ),
    )(*operands)


def cut_kernel(*refs):
    count = len(refs) - 3
    images, (within, across, sems) = refs[:count], refs[count:]
    last = images[0].shape[0] - 1
    even = lax.axis_index("space") % 2 == 0

    def copies(inner, outer):
        moves = []
        for k, image in enumerate(images):
            moves.append(pltpu.make_async_copy(image.at[inner], within.at[k], sems.at[2 * k]))
            moves.append(pltpu.make_async_copy(image.at[outer], across.at[k], sems.at[2 * k + 1]))
        return moves

    pl.when(even)(lambda: [c.start() for c in copies(last, 0)] and None)
    pl.when(jnp.logical_not(even))(lambda: [c.start() for c in copies(0, last)] and None)
    for c in copies(last, 0):
        c.wait()


def cut(images):
    count = len(images)
    block = (count,) + images[0].shape[1:]
    return pl.pallas_call(
        cut_kernel,
        in_specs=[pl.BlockSpec(memory_space=pl.ANY)] * count,
        out_specs=[pl.BlockSpec(memory_space=pltpu.VMEM)] * 2,
        out_shape=[jax.ShapeDtypeStruct(block, jnp.float32)] * 2,
        scratch_shapes=[pltpu.SemaphoreType.DMA((2 * count,))],
        compiler_params=pltpu.CompilerParams(vmem_limit_bytes=6 << 20),
        cost_estimate=pl.CostEstimate(flops=0, bytes_accessed=16 * count * block[1] * block[2], transcendentals=0),
    )(*images)


def settle_kernel(terms, slices, kept, origin, total, *refs):
    refs = list(refs)
    take = lambda k: [refs.pop(0) for _ in range(k)]
    duals = [take(len(starts)) for starts in terms]
    weights, gains = take(len(terms)), take(len(terms))
    finished = [z for z in slices if z not in kept]
    if finished:
        out, sems = refs[-2:]
        del refs[-2:]
        result = refs.pop()
    rest = refs[-1] if kept else None
    rows = total.shape[1]
    moves = []
    for z in finished + list(kept):
        here_terms = []
        for k, starts in enumerate(terms):
            for piece, start in enumerate(starts):
                if start <= z < start + duals[k][piece].shape[0]:
                    here_terms.append((duals[k][piece], z - start, weights[k], gains[k]))
        place = kept.index(z) if z in kept else finished.index(z)
        target = rest if z in kept else out

        def body(step, carry):
            here = pl.ds(pl.multiple_of(step * SETTLE, SETTLE), SETTLE)
            arriving = None
            for dual, within, weight, gain in here_terms:
                value = dual[within, here, :] + gain[z, here, :]
                value = weight[z, here, :] * jnp.minimum(jnp.maximum(value, -dual_bound), dual_bound)
                arriving = value if arriving is None else arriving + value
            target[place, here, :] = total[z - origin, here, :] - flow * arriving
            return carry

        lax.fori_loop(0, rows // SETTLE, body, 0)
        if z not in kept:
            moves.append(pltpu.make_async_copy(out.at[place], result.at[z], sems.at[place]))
            moves[-1].start()
    for m in moves:
        m.wait()


def settle(total, terms, slices, kept, depth, result=None, origin=0):
    vmem_spec, any_spec = pl.BlockSpec(memory_space=pltpu.VMEM), pl.BlockSpec(memory_space=pl.ANY)
    rows, columns = total.shape[1:]
    f32 = jnp.float32
    operands = [total, *(d for t in terms for d in t[0]), *(t[2] for t in terms), *(t[3] for t in terms)]
    specs = [vmem_spec] * len(operands)
    finished = len(slices) - len(kept)
    aliases = {}
    if result is not None:
        aliases = {len(operands): 0}
        operands.append(result)
        specs.append(any_spec)
    shapes, out_specs, scratch = [], [], []
    if kept:
        shapes.append(jax.ShapeDtypeStruct((len(kept), rows, columns), f32))
        out_specs.append(vmem_spec)
    if finished:
        shapes.append(jax.ShapeDtypeStruct((depth, rows, columns), f32))
        out_specs.append(any_spec)
        scratch = [pltpu.VMEM((finished, rows, columns), f32), pltpu.SemaphoreType.DMA((finished,))]
    return pl.pallas_call(
        functools.partial(settle_kernel, tuple(t[1] for t in terms), slices, kept, origin),
        in_specs=specs,
        out_specs=out_specs,
        out_shape=shapes,
        input_output_aliases=aliases,
        scratch_shapes=scratch,
        compiler_params=pltpu.CompilerParams(vmem_limit_bytes=10 << 20),
        cost_estimate=pl.CostEstimate(
            flops=5 * len(terms) * total.size, bytes_accessed=4 * (2 + 3 * len(terms)) * total.size, transcendentals=0
        ),
    )(*operands)


def complete(pairs_, frames, spaces):
    return [
        (a * spaces + s, b * spaces + s if 0 <= b < frames else a * spaces + (s ^ 1))
        for a, b in pairs_
        for s in range(spaces)
    ]


def shards(volume, prior_image, dual_pairs, pair_cycle, pair_offset):
    frames = lax.axis_size("tm")
    spaces = lax.axis_size("space")
    stride = frames // CYCLES
    image = volume[0]
    dual = dual_pairs[0]
    cycle_of = lambda t: t // stride
    every = range(frames)
    swap = [(t, t + stride if cycle_of(t) % 2 == 0 else t - stride) for t in every]
    cross = [(t, t - stride if cycle_of(t) % 2 == 0 else t + stride) for t in every]
    cross = complete(cross, frames, spaces)
    wide_swap = [(t, t + 2 * stride if cycle_of(t) // 2 % 2 == 0 else t - 2 * stride) for t in every]
    wide_cross = [(t, t - 2 * stride if cycle_of(t) // 2 % 2 == 0 else t + 2 * stride) for t in every]
    wide_cross = complete(wide_cross, frames, spaces)
    relay = [(t, t + 2 * stride if cycle_of(t) % 2 == 0 else t - 2 * stride) for t in every]
    relay = [(a, b) for a, b in relay if 0 <= b < frames]
    inner = [(s, s ^ 1) for s in range(spaces)]
    outer = [(s, s - 1 if s % 2 == 0 else s + 1) for s in range(spaces)]
    outer = [(a, b) for a, b in outer if 0 <= b < spaces]

    def send(x, pairs_, axis="tm"):
        return lax.ppermute(x, axis, pairs_)

    table = jnp.concatenate([pair_cycle[0], pair_offset[0]])

    def halos(images):
        within, across = cut(images)
        return send(within, inner, "space"), send(across, outer, "space")

    near_image = send(image, swap)
    wide_near_image = send(image, wide_swap)
    wide_far_image = send(image, wide_cross, ("tm", "space"))
    near_table = send(table, swap)
    far_table = send(table, cross, ("tm", "space"))
    wide_near_table = send(table, wide_swap)
    wide_far_table = send(table, wide_cross, ("tm", "space"))
    depth = image.shape[0]
    part = max(depth // 4, 1)
    both = ("tm", "space")
    near_main, near_last, far_main, far_last = pack((0, 1), ((depth - part, part),) * 2, stride, table, dual)
    near_main = send(near_main, swap)
    far_main = send(far_main, cross, both)
    lead, rest, wide_last, far_lead, main, last = pack(
        (2, 3), ((part, depth - 2 * part, part),) * 2, stride, table, dual
    )
    lead = send(lead, wide_swap)
    far_lead = send(far_lead, wide_cross, ("tm", "space"))
    far_image = send(near_image, relay)

    within, across = halos((image, near_image, wide_near_image, wide_far_image))
    main = send(main, wide_cross, ("tm", "space"))
    rest = send(rest, wide_swap)
    near_last = send(near_last, swap)
    far_last = send(far_last, cross, both)
    last = send(last, wide_cross, ("tm", "space"))
    wide_last = send(wide_last, wide_swap)
    fresh, total, w0, w2, w3, g0, g2, g3 = pairs(
        ((0, 1), (2, 2), (3, 3)), stride, table, (near_table, wide_near_table, wide_far_table),
        image, dual, prior_image[0],
        (near_image, wide_near_image, wide_far_image), (within,) * 3, (across,) * 3, (within, across),
    )
    far_within, far_across = halos((far_image,))
    fresh, total, w1, g1 = pairs(
        ((1, 0),), stride, table, (far_table,), image, dual, total,
        (far_image,), (far_within,), (far_across,), (within, across), fresh,
    )
    early, late = tuple(range(depth - part)), tuple(range(depth - part, depth))
    start = depth - part
    (volume_next,) = settle(
        total,
        (
            ((near_main,), (0,), w0, g0),
            ((far_main,), (0,), w1, g1),
            ((lead, rest), (0, part), w2, g2),
            ((far_lead, main), (0, part), w3, g3),
        ),
        early, (), depth,
    )
    (volume_next,) = settle(
        total,
        (
            ((near_last,), (start,), w0, g0),
            ((far_last,), (start,), w1, g1),
            ((wide_last,), (start,), w2, g2),
            ((last,), (start,), w3, g3),
        ),
        late, (), depth, volume_next,
    )
    return (volume_next[None], fresh[None])


def solution(mesh):
    return jax.shard_map(
        shards,
        mesh=mesh,
        in_specs=(
            P("tm", "space", None, None),
            P("tm", "space", None, None),
            P("tm", None, "space", None, None),
            P("tm", None),
            P("tm", None),
        ),
        out_specs=(P("tm", "space", None, None), P("tm", None, "space", None, None)),
        check_vma=False,
    )
```

```python
import functools

import jax
import jax.numpy as jnp
from jax import lax
from jax.experimental import pallas as pl
from jax.experimental.pallas import tpu as pltpu
from jax.sharding import PartitionSpec as P


CYCLES = 8
HOPS = (-2, -1, 1, 2)

dual_step = 0.5
primal_step = 0.25
dual_bound = 0.3
fidelity = 1.0
scale = 1.0 / (1.0 + primal_step * fidelity)
flow = primal_step * scale
patch = -1.0 / (27.0 * 4.0)


LANES = 128
STEP = 64
SETTLE = 128
PARTS = 2
EDGE = 16
RIM = 8


def chosen(table, hop):
    slot = jnp.int32(0)
    filled = table[0] == hop
    for k in range(1, 4):
        hit = table[k] == hop
        slot = jnp.where(hit, k, slot)
        filled = filled | hit
    return slot, filled


def offset_of(table, hop):
    offset = jnp.int32(0)
    for k in range(4):
        offset = jnp.where(table[k] == hop, table[4 + k], offset)
    return offset


def home_slot(table, hop):
    slot, filled = chosen(table, hop)
    count = jnp.int32(0)
    for k in range(4):
        count = count + (table[k] != 0).astype(jnp.int32)
    for other in HOPS:
        _, other_filled = chosen(table, other)
        count = count + ((other < hop) & jnp.logical_not(other_filled)).astype(jnp.int32)
    return jnp.where(filled, slot, count), filled


def hop_of(place, stride):
    width = 1 if place < 2 else 2
    parity = (lax.axis_index("tm") // (stride * width)) % 2
    near = (width * (1 - 2 * parity)).astype(jnp.int32)
    return near if place % 2 == 0 else -near


def piece_of(pieces, z):
    for piece, size in enumerate(pieces):
        if z < size:
            return piece, z
        z -= size


def pack_kernel(places, pieces, stride, table, dual, *refs):
    count = len(places)
    held, sems = refs[-2:]
    refs = list(refs[:-2])
    outs = [[refs.pop(0) for _ in some] for some in pieces]
    depth, rows = dual.shape[1:3]
    moves = []
    for j, place in enumerate(places):
        slot, _ = chosen(table, hop_of(place, stride))
        for half in range(2):
            source = dual.at[slot, :, :, pl.ds(half * LANES, LANES)]
            moves.append(
                pltpu.make_async_copy(source, held.at[j, :, half, pl.ds(RIM, rows), :], sems.at[2 * j + half])
            )
    for m in moves:
        m.start()
    for j in range(count):
        for z in range(depth):
            for half in range(2):
                held[j, z, half, pl.ds(0, RIM), :] = jnp.zeros((RIM, LANES), jnp.float32)
                held[j, z, half, pl.ds(RIM + rows, RIM), :] = jnp.zeros((RIM, LANES), jnp.float32)
    for j, place in enumerate(places):
        offset = offset_of(table, hop_of(place, stride))
        moves[2 * j].wait()
        moves[2 * j + 1].wait()

        def body(step, carry):
            y = pl.multiple_of(step * STEP, STEP)
            for z in range(depth):
                for half in range(2):
                    piece, within = piece_of(pieces[j], z)
                    outs[j][piece][within, pl.ds(y, STEP), pl.ds(half * LANES, LANES)] = held[
                        j, z, half, pl.ds(RIM + y + offset, STEP), :
                    ]
            return carry

        lax.fori_loop(0, rows // STEP, body, 0)


def pack(places, pieces, stride, table, dual):
    _, depth, rows, columns = dual.shape
    count = len(places)
    return pl.pallas_call(
        functools.partial(pack_kernel, places, pieces, stride),
        in_specs=[pl.BlockSpec(memory_space=pltpu.SMEM), pl.BlockSpec(memory_space=pltpu.HBM)],
        out_specs=[pl.BlockSpec(memory_space=pltpu.VMEM)] * sum(map(len, pieces)),
        out_shape=[jax.ShapeDtypeStruct((size, rows, columns), jnp.float32) for some in pieces for size in some],
        scratch_shapes=[
            pltpu.VMEM((count, depth, 2, rows + 2 * RIM, LANES), jnp.float32),
            pltpu.SemaphoreType.DMA((2 * count,)),
        ],
        compiler_params=pltpu.CompilerParams(vmem_limit_bytes=8 << 20),
        cost_estimate=pl.CostEstimate(
            flops=0, bytes_accessed=2 * count * 4 * depth * rows * columns, transcendentals=0
        ),
    )(table, pltpu.with_memory_space_constraint(dual, pltpu.HBM))


def box_rows(sums, z, half, start):
    return (
        sums[z, half, pl.ds(start - 1, STEP), :]
        + sums[z, half, pl.ds(start, STEP), :]
        + sums[z, half, pl.ds(start + 1, STEP), :]
    )


def box_lanes(left, right, lane):
    zero = jnp.zeros_like(left)
    left_up, right_up = pltpu.roll(left, 1, 1), pltpu.roll(right, 1, 1)
    left_down, right_down = pltpu.roll(left, LANES - 1, 1), pltpu.roll(right, LANES - 1, 1)
    first, last = lane == 0, lane == LANES - 1
    return (
        left + jnp.where(first, zero, left_up) + jnp.where(last, right_down, left_down),
        right + jnp.where(first, left_up, right_up) + jnp.where(last, zero, right_down),
    )


def pair_kernel(places, first, stride, table, *refs):
    count = len(places)
    refs = list(refs)
    take = lambda k: [refs.pop(0) for _ in range(k)]
    tables = take(count)
    image, dual, start = take(3)
    partners, inner, outer, own_halos = take(count), take(count), take(count), take(2)
    if not first:
        take(1)
    fresh_out, total = take(2)
    weights, gains = take(count), take(count)
    held, rim, own_sums, in_sums, fresh, sems, out_sems = refs
    depth, rows, _ = image.shape
    f32 = jnp.float32

    even = lax.axis_index("space") % 2 == 0

    def copies(i, upper, lower):
        stacked = places[i][1]
        moves = []
        for half in range(2):
            lanes = pl.ds(half * LANES, LANES)
            moves.append((partners[i].at[:, :, lanes], held.at[i, pl.ds(1, depth), half, pl.ds(EDGE, rows), :]))
            moves.append((upper.at[stacked, :, lanes], held.at[i, 0, half, pl.ds(EDGE, rows), :]))
            moves.append((lower.at[stacked, :, lanes], held.at[i, depth + 1, half, pl.ds(EDGE, rows), :]))
        return [pltpu.make_async_copy(a, b, sems.at[6 * i + j]) for j, (a, b) in enumerate(moves)]

    def start_all(uppers, lowers, own_upper, own_lower):
        for c in rim_copies(own_upper, own_lower):
            c.start()
        for i in range(count):
            for c in copies(i, uppers[i], lowers[i]):
                c.start()

    def rim_copies(upper, lower):
        return [
            pltpu.make_async_copy(upper.at[0], rim.at[0], sems.at[6 * count]),
            pltpu.make_async_copy(lower.at[0], rim.at[1], sems.at[6 * count + 1]),
        ]

    pl.when(even)(lambda: start_all(outer, inner, own_halos[1], own_halos[0]))
    pl.when(jnp.logical_not(even))(lambda: start_all(inner, outer, own_halos[0], own_halos[1]))
    in_copies = [copies(i, inner[i], outer[i]) for i in range(count)]
    for i in range(count):
        for z in range(depth + 2):
            for half in range(2):
                held[i, z, half, pl.ds(0, EDGE), :] = jnp.zeros((EDGE, LANES), f32)
                held[i, z, half, pl.ds(EDGE + rows, EDGE), :] = jnp.zeros((EDGE, LANES), f32)
    for z in range(depth):
        for half in range(2):
            own_sums[z, half, pl.ds(0, RIM), :] = jnp.zeros((RIM, LANES), f32)
            own_sums[z, half, pl.ds(RIM + rows, RIM), :] = jnp.zeros((RIM, LANES), f32)

    row = lax.broadcasted_iota(jnp.int32, (STEP, LANES), 0)
    lane = lax.broadcasted_iota(jnp.int32, (STEP, LANES), 1)

    def mine(z, half, y):
        here, lanes = pl.ds(pl.multiple_of(y, 8), STEP), pl.ds(half * LANES, LANES)
        if z == 0:
            return rim[0, here, lanes]
        if z == depth + 1:
            return rim[1, here, lanes]
        return image[z - 1, here, lanes]

    def store_sums(sums, half, y, size, squares):
        for z in range(depth):
            sums[z, half, pl.ds(pl.multiple_of(RIM + y, 8), size), :] = squares[z] + squares[z + 1] + squares[z + 2]

    for c in rim_copies(*own_halos):
        c.wait()
    out_copies = []
    for i in range(count):
        hop = hop_of(places[i][0], stride)
        source, _ = chosen(table, hop)
        own_offset = offset_of(table, hop)
        slot, filled = home_slot(table, hop)
        bound = jnp.where(filled, f32(dual_bound), f32(0.0))
        _, in_filled = chosen(tables[i], -hop)
        partner = lax.axis_index("tm") // stride + hop
        in_filled = in_filled & (partner >= 0) & (partner < CYCLES)
        in_offset = offset_of(tables[i], -hop)
        low = jnp.where(in_filled, -in_offset, 4 * rows)
        high = rows - 1 - in_offset
        for c in in_copies[i]:
            c.wait()

        def theirs(z, half, y, shift, size=STEP):
            return held[i, z, half, pl.ds(EDGE + y + shift, size), :]

        for y in (-RIM, rows):
            for half in range(2):
                values = [theirs(z, half, y, in_offset, RIM) for z in range(depth + 2)]
                store_sums(in_sums, half, y, RIM, [v * v for v in values])

        def gather(step, carry):
            y = pl.multiple_of(step * STEP, STEP)
            inside = (row + y >= low) & (row + y <= high)
            for half in range(2):
                own_squares, in_squares = [], []
                for z in range(depth + 2):
                    value = mine(z, half, y)
                    own_square = theirs(z, half, y, -own_offset) - value
                    own_squares.append(own_square * own_square)
                    in_square = jnp.where(inside, value, 0.0) - theirs(z, half, y, in_offset)
                    in_squares.append(in_square * in_square)
                store_sums(own_sums, half, y, STEP, own_squares)
                store_sums(in_sums, half, y, STEP, in_squares)
            return carry

        def apply(step, carry):
            y = pl.multiple_of(step * STEP, STEP)
            inside = (row + y >= low) & (row + y <= high)
            here = pl.ds(y, STEP)
            for z in range(depth):
                own_box = box_lanes(box_rows(own_sums, z, 0, RIM + y), box_rows(own_sums, z, 1, RIM + y), lane)
                in_box = box_lanes(box_rows(in_sums, z, 0, RIM + y), box_rows(in_sums, z, 1, RIM + y), lane)
                for half in range(2):
                    lanes = pl.ds(half * LANES, LANES)
                    value = mine(z + 1, half, y)
                    weight = jnp.exp(own_box[half] * patch)
                    contrast = theirs(z + 1, half, y, -own_offset) - value
                    step_to = dual[source, z, here, lanes] + (dual_step * weight) * contrast
                    step_to = jnp.minimum(jnp.maximum(step_to, -bound), bound)
                    fresh[i, z, here, lanes] = step_to
                    flux = (weight * step_to) * flow
                    if i > 0:
                        total[z, here, lanes] = total[z, here, lanes] + flux
                    elif first:
                        total[z, here, lanes] = scale * value + (flow * fidelity) * start[z, here, lanes] + flux
                    else:
                        total[z, here, lanes] = start[z, here, lanes] + flux
                    weight = jnp.exp(in_box[half] * patch)
                    weights[i][z, here, lanes] = jnp.where(inside, weight, 0.0)
                    gains[i][z, here, lanes] = (dual_step * weight) * (value - theirs(z + 1, half, y, in_offset))
            return carry

        steps = rows // STEP
        lax.fori_loop(0, steps, gather, 0)
        for part in range(PARTS):
            lax.fori_loop(part * steps // PARTS, (part + 1) * steps // PARTS, apply, 0)
            some = pl.ds(part * rows // PARTS, rows // PARTS)
            done = pltpu.make_async_copy(
                fresh.at[i, :, some, :], fresh_out.at[slot, :, some, :], out_sems.at[PARTS * i + part]
            )
            done.start()
            out_copies.append(done)
    for c in out_copies:
        c.wait()


def pairs(places, stride, table, tables, image, dual, start, partners, inner, outer, own_halos, fresh=None):
    count = len(places)
    depth, rows, columns = image.shape
    first = fresh is None
    f32 = jnp.float32
    block = jax.ShapeDtypeStruct(image.shape, f32)
    any_spec = pl.BlockSpec(memory_space=pl.ANY)
    vmem_spec = pl.BlockSpec(memory_space=pltpu.VMEM)
    smem = pl.BlockSpec(memory_space=pltpu.SMEM)
    operands = [table, *tables, image, dual, start, *partners, *inner, *outer, *own_halos]
    specs = [smem] * (1 + count) + [vmem_spec] * 3 + [any_spec] * (3 * count + 2)
    aliases = {}
    if not first:
        aliases = {len(operands): 0}
        operands.append(fresh)
        specs.append(any_spec)
    cells = depth * rows * columns
    return pl.pallas_call(
        functools.partial(pair_kernel, places, first, stride),
        in_specs=specs,
        out_specs=[any_spec] + [vmem_spec] * (1 + 2 * count),
        out_shape=[jax.ShapeDtypeStruct(dual.shape, f32)] + [block] * (1 + 2 * count),
        input_output_aliases=aliases,
        scratch_shapes=[
            pltpu.VMEM((count, depth + 2, 2, rows + 2 * EDGE, LANES), f32),
            pltpu.VMEM((2, rows, columns), f32),
            pltpu.VMEM((depth, 2, rows + 2 * RIM, LANES), f32),
            pltpu.VMEM((depth, 2, rows + 2 * RIM, LANES), f32),
            pltpu.VMEM((count, depth, rows, columns), f32),
            pltpu.SemaphoreType.DMA((6 * count + 2,)),
            pltpu.SemaphoreType.DMA((PARTS * count,)),
        ],
        compiler_params=pltpu.CompilerParams(vmem_limit_bytes=20 << 20),
        cost_estimate=pl.CostEstimate(
            flops=count * 60 * cells, bytes_accessed=4 * (3 + 7 * count) * cells, transcendentals=2 * count * cells
        ),
    )(*operands)


def cut_kernel(*refs):
    count = len(refs) - 3
    images, (within, across, sems) = refs[:count], refs[count:]
    last = images[0].shape[0] - 1
    even = lax.axis_index("space") % 2 == 0

    def copies(inner, outer):
        moves = []
        for k, image in enumerate(images):
            moves.append(pltpu.make_async_copy(image.at[inner], within.at[k], sems.at[2 * k]))
            moves.append(pltpu.make_async_copy(image.at[outer], across.at[k], sems.at[2 * k + 1]))
        return moves

    pl.when(even)(lambda: [c.start() for c in copies(last, 0)] and None)
    pl.when(jnp.logical_not(even))(lambda: [c.start() for c in copies(0, last)] and None)
    for c in copies(last, 0):
        c.wait()


def cut(images):
    count = len(images)
    block = (count,) + images[0].shape[1:]
    return pl.pallas_call(
        cut_kernel,
        in_specs=[pl.BlockSpec(memory_space=pl.ANY)] * count,
        out_specs=[pl.BlockSpec(memory_space=pltpu.VMEM)] * 2,
        out_shape=[jax.ShapeDtypeStruct(block, jnp.float32)] * 2,
        scratch_shapes=[pltpu.SemaphoreType.DMA((2 * count,))],
        compiler_params=pltpu.CompilerParams(vmem_limit_bytes=6 << 20),
        cost_estimate=pl.CostEstimate(flops=0, bytes_accessed=16 * count * block[1] * block[2], transcendentals=0),
    )(*images)


def settle_kernel(terms, slices, kept, origin, total, *refs):
    refs = list(refs)
    take = lambda k: [refs.pop(0) for _ in range(k)]
    duals = [take(len(starts)) for starts in terms]
    weights, gains = take(len(terms)), take(len(terms))
    finished = [z for z in slices if z not in kept]
    if finished:
        out, sems = refs[-2:]
        del refs[-2:]
        result = refs.pop()
    rest = refs[-1] if kept else None
    rows = total.shape[1]
    moves = []
    for z in finished + list(kept):
        here_terms = []
        for k, starts in enumerate(terms):
            for piece, start in enumerate(starts):
                if start <= z < start + duals[k][piece].shape[0]:
                    here_terms.append((duals[k][piece], z - start, weights[k], gains[k]))
        place = kept.index(z) if z in kept else finished.index(z)
        target = rest if z in kept else out

        def body(step, carry):
            here = pl.ds(pl.multiple_of(step * SETTLE, SETTLE), SETTLE)
            arriving = None
            for dual, within, weight, gain in here_terms:
                value = dual[within, here, :] + gain[z, here, :]
                value = weight[z, here, :] * jnp.minimum(jnp.maximum(value, -dual_bound), dual_bound)
                arriving = value if arriving is None else arriving + value
            target[place, here, :] = total[z - origin, here, :] - flow * arriving
            return carry

        lax.fori_loop(0, rows // SETTLE, body, 0)
        if z not in kept:
            moves.append(pltpu.make_async_copy(out.at[place], result.at[z], sems.at[place]))
            moves[-1].start()
    for m in moves:
        m.wait()


def settle(total, terms, slices, kept, depth, result=None, origin=0):
    vmem_spec, any_spec = pl.BlockSpec(memory_space=pltpu.VMEM), pl.BlockSpec(memory_space=pl.ANY)
    rows, columns = total.shape[1:]
    f32 = jnp.float32
    operands = [total, *(d for t in terms for d in t[0]), *(t[2] for t in terms), *(t[3] for t in terms)]
    specs = [vmem_spec] * len(operands)
    finished = len(slices) - len(kept)
    aliases = {}
    if result is not None:
        aliases = {len(operands): 0}
        operands.append(result)
        specs.append(any_spec)
    shapes, out_specs, scratch = [], [], []
    if kept:
        shapes.append(jax.ShapeDtypeStruct((len(kept), rows, columns), f32))
        out_specs.append(vmem_spec)
    if finished:
        shapes.append(jax.ShapeDtypeStruct((depth, rows, columns), f32))
        out_specs.append(any_spec)
        scratch = [pltpu.VMEM((finished, rows, columns), f32), pltpu.SemaphoreType.DMA((finished,))]
    return pl.pallas_call(
        functools.partial(settle_kernel, tuple(t[1] for t in terms), slices, kept, origin),
        in_specs=specs,
        out_specs=out_specs,
        out_shape=shapes,
        input_output_aliases=aliases,
        scratch_shapes=scratch,
        compiler_params=pltpu.CompilerParams(vmem_limit_bytes=10 << 20),
        cost_estimate=pl.CostEstimate(
            flops=5 * len(terms) * total.size, bytes_accessed=4 * (2 + 3 * len(terms)) * total.size, transcendentals=0
        ),
    )(*operands)


def complete(pairs_, frames, spaces):
    return [
        (a * spaces + s, b * spaces + s if 0 <= b < frames else a * spaces + (s ^ 1))
        for a, b in pairs_
        for s in range(spaces)
    ]


def shards(volume, prior_image, dual_pairs, pair_cycle, pair_offset):
    frames = lax.axis_size("tm")
    spaces = lax.axis_size("space")
    stride = frames // CYCLES
    image = volume[0]
    dual = dual_pairs[0]
    cycle_of = lambda t: t // stride
    every = range(frames)
    swap = [(t, t + stride if cycle_of(t) % 2 == 0 else t - stride) for t in every]
    cross = [(t, t - stride if cycle_of(t) % 2 == 0 else t + stride) for t in every]
    cross = complete(cross, frames, spaces)
    wide_swap = [(t, t + 2 * stride if cycle_of(t) // 2 % 2 == 0 else t - 2 * stride) for t in every]
    wide_cross = [(t, t - 2 * stride if cycle_of(t) // 2 % 2 == 0 else t + 2 * stride) for t in every]
    wide_cross = complete(wide_cross, frames, spaces)
    relay = [(t, t + 2 * stride if cycle_of(t) % 2 == 0 else t - 2 * stride) for t in every]
    relay = [(a, b) for a, b in relay if 0 <= b < frames]
    inner = [(s, s ^ 1) for s in range(spaces)]
    outer = [(s, s - 1 if s % 2 == 0 else s + 1) for s in range(spaces)]
    outer = [(a, b) for a, b in outer if 0 <= b < spaces]

    def send(x, pairs_, axis="tm"):
        return lax.ppermute(x, axis, pairs_)

    table = jnp.concatenate([pair_cycle[0], pair_offset[0]])

    def halos(images):
        within, across = cut(images)
        return send(within, inner, "space"), send(across, outer, "space")

    near_image = send(image, swap)
    wide_near_image = send(image, wide_swap)
    wide_far_image = send(image, wide_cross, ("tm", "space"))
    near_table = send(table, swap)
    far_table = send(table, cross, ("tm", "space"))
    wide_near_table = send(table, wide_swap)
    wide_far_table = send(table, wide_cross, ("tm", "space"))
    depth = image.shape[0]
    part = max(depth // 4, 1)
    near_dual, far_dual = pack((0, 1), ((depth,),) * 2, stride, table, dual)
    near_dual = send(near_dual, swap)
    far_dual = send(far_dual, cross, ("tm", "space"))
    lead, rest, near_last, far_lead, main, last = pack(
        (2, 3), ((part, depth - 2 * part, part),) * 2, stride, table, dual
    )
    lead = send(lead, wide_swap)
    far_lead = send(far_lead, wide_cross, ("tm", "space"))
    far_image = send(near_image, relay)

    within, across = halos((image, near_image, wide_near_image, wide_far_image))
    main = send(main, wide_cross, ("tm", "space"))
    rest = send(rest, wide_swap)
    last = send(last, wide_cross, ("tm", "space"))
    near_last = send(near_last, wide_swap)
    fresh, total, w0, w2, w3, g0, g2, g3 = pairs(
        ((0, 1), (2, 2), (3, 3)), stride, table, (near_table, wide_near_table, wide_far_table),
        image, dual, prior_image[0],
        (near_image, wide_near_image, wide_far_image), (within,) * 3, (across,) * 3, (within, across),
    )
    far_within, far_across = halos((far_image,))
    fresh, total, w1, g1 = pairs(
        ((1, 0),), stride, table, (far_table,), image, dual, total,
        (far_image,), (far_within,), (far_across,), (within, across), fresh,
    )
    every_slice, early, late = tuple(range(depth)), tuple(range(depth - part)), tuple(range(depth - part, depth))
    (total,) = settle(
        total, (((near_dual,), (0,), w0, g0), ((far_dual,), (0,), w1, g1)), every_slice, every_slice, depth
    )
    (volume_next,) = settle(
        total, (((lead, rest), (0, part), w2, g2), ((far_lead, main), (0, part), w3, g3)), early, (), depth
    )
    (volume_next,) = settle(
        total,
        (((near_last,), (depth - part,), w2, g2), ((last,), (depth - part,), w3, g3)), late, (), depth, volume_next,
    )
    return (volume_next[None], fresh[None])


def solution(mesh):
    return jax.shard_map(
        shards,
        mesh=mesh,
        in_specs=(
            P("tm", "space", None, None),
            P("tm", "space", None, None),
            P("tm", None, "space", None, None),
            P("tm", None),
            P("tm", None),
        ),
        out_specs=(P("tm", "space", None, None), P("tm", None, "space", None, None)),
        check_vma=False,
    )
```
